32 devices in a mesh: clips: 2 (over x), gx: 4 (over y, core), gy: 4 (over z).
Axes of the slice: x: 2, y: 2, z: 4, core: 2. Of those that a mesh axis runs over, the one named last changes fastest.
Arguments:
- fields: float32 [12, 32, 32, 512], P('clips', None, 'gx', 'gy'), parts along dimension 0, may hold values from -6 to 6
- material_map: int32 [64, 32, 512], P('clips', 'gx', 'gy'), parts along dimension 0, may hold values from 0 to 3
- material_eps: float32 [4], replicated, may hold values from 1 to 4
- material_loss: float32 [4], replicated, may hold values from 0 to 0.4
- source_shift: int32 [64, 2], P(('gx', 'gy')), may hold values from -8 to 8
- source_mask: int32 [64, 96, 96], P(('gx', 'gy')), may hold values 0 or 1
- source_weight: float32 [64], P(('gx', 'gy')), may hold values from 0.25 to 4
Outputs:
- final_fields: float32 [12, 32, 32, 512], P('clips', None, 'gx', 'gy'), parts along dimension 0
- image: float32 [512, 1024], P(('gx', 'gy'), 'clips'), parts along dimension 1
The draws below stay inside these ranges and needn't reach their ends.
There are 2 independent parts, one for each index of `clips`. The reference program is written for one: setup_inputs(seed, part) draws one part's arguments, and reference() takes and returns one part's arrays. A program takes and returns all parts, laid end to end along the dimension named above; an argument that names none is the same for every part. Nothing has to cross between parts.
All inputs are finite; a program needn't handle non-finite values. No bound on the sum of `source_mask` on one device may be relied on, other than what follows from the above.
Results may differ from the reference program's by a relative error of at most 0.0014.
The reference program's roundings to bfloat16 on the way (of `orders_b`, `masked` and `columns`) count: a program that leaves them out, or rounds other values in their place, can miss the bound.
Values sent between devices are 32-bit elements; how exact they have to be, the bound alone decides.
No kernel may reach another device: no remote copies, remote signals or barrier semaphores. Data moves between devices by JAX's collectives and lax.ppermute only.
A program may use at most 64 MiB of HBM per device.

```python
import math
import jax
import jax.numpy as jnp
from jax import lax

NZ = 32
STEPS = 12
MATS = 4
P_SIZE = 96
Q = 96
M = 512
NX = 32
NY = 512
SOURCES = 64


def plant(entries, rng, low, top_value):
    place = [jax.random.randint(jax.random.fold_in(rng, axis), (), 0, length) for axis, length in enumerate(entries.shape)]
    widest = entries.shape.index(max(entries.shape))
    beside = place[:widest] + [(place[widest] + 1) % entries.shape[widest]] + place[widest + 1:]
    return entries.at[tuple(place)].set(low).at[tuple(beside)].set(top_value)


def block_scale(key, shape, pieces, low, top_value):
    gain, own = 1.0, jax.random.fold_in(key, 6)
    for dim, parts in pieces:
        heights = jnp.exp(jax.random.uniform(jax.random.fold_in(own, dim), (parts,), jnp.float32, low / len(pieces), top_value / len(pieces)))
        gain = gain * jnp.repeat(heights, shape[dim] // parts).reshape([-1 if axis == dim else 1 for axis in range(len(shape))])
    return gain


def scatter_about(own_key, shape, deviation, most, pieces=(), kind=jnp.bfloat16):
    result = jax.random.normal(own_key, shape, jnp.float32) * deviation
    if len(pieces) > 0:
        result = block_scale(own_key, shape, pieces, -0.22, 0.18) * result
    return jnp.clip(result, min=-most, max=most).astype(kind)


def setup_inputs(seed: int = 0, part: int = 0) -> dict:
    keys = jax.random.split(jax.random.key(seed), 8)
    part_keys = jax.random.split(jax.random.fold_in(keys[7], part), 8)
    fields = scatter_about(part_keys[0], (6, NZ, NX, NY), 1.0, 6.0, ((2, 4), (3, 4)), jnp.float32)
    material_map = plant(jax.random.randint(part_keys[1], (NZ, NX, NY), 0, MATS), jax.random.fold_in(part_keys[1], 1), 0, MATS - 1).astype(jnp.int32)
    material_eps = jnp.clip(jnp.exp(jax.random.uniform(keys[2], (MATS,), jnp.float32, math.log(1.0), math.log(4.0))), 1.0, 4.0)
    material_loss = jnp.clip(jax.random.uniform(keys[3], (MATS,), jnp.float32, 0.0, 0.4), 0.0, 0.4)
    source_shift = plant(jax.random.randint(keys[4], (SOURCES, 2), -8, 9), jax.random.fold_in(keys[4], 1), -8, 8).astype(jnp.int32)
    source_mask = plant((jax.random.randint(keys[5], (SOURCES, P_SIZE, Q), 0, 4) < 3).astype(jnp.int32), jax.random.fold_in(keys[5], 1), 0, 1)
    source_weight = jnp.clip(jnp.exp(math.log(4.0) - 2.7725887 * jax.random.uniform(keys[6], (SOURCES,), jnp.float32) ** block_scale(keys[6], (SOURCES,), ((0, 16),), -0.2, 0.2)), 0.25, 4.0)
    return dict(fields=fields, material_map=material_map, material_eps=material_eps, material_loss=material_loss, source_shift=source_shift, source_mask=source_mask, source_weight=source_weight)


COURANT = 0.55
ANGULAR = 0.7
PRECISE = lax.Precision.HIGHEST

def ahead(values, dimension, border):
    remainder = lax.slice_in_dim(values, 1, values.shape[dimension], axis=dimension)
    return jnp.concatenate((remainder, border), dimension)

def behind(values, dimension, border):
    remainder = lax.slice_in_dim(values, 0, values.shape[dimension] - 1, axis=dimension)
    return jnp.concatenate((border, remainder), dimension)

def blank(values, dimension):
    extent = list(values.shape)
    extent[dimension] = 1
    return jnp.zeros(extent, values.dtype)

def magnetic(efield, hfield, borders):

    def change(component, dimension):
        border = borders.get((component, dimension))
        if border is None:
            border = blank(efield[component], dimension)
        return ahead(efield[component], dimension, border) - efield[component]
    new_x = hfield[0] - COURANT * (change(2, 2) - change(1, 0))
    new_y = hfield[1] - COURANT * (change(0, 0) - change(2, 1))
    new_z = hfield[2] - COURANT * (change(1, 1) - change(0, 2))
    return (new_x, new_y, new_z)

def electric(efield, hfield, coef_keep, coef_curl, borders):

    def change(component, dimension):
        border = borders.get((component, dimension))
        if border is None:
            border = blank(hfield[component], dimension)
        return hfield[component] - behind(hfield[component], dimension, border)
    new_x = coef_keep * efield[0] + coef_curl * (change(2, 2) - change(1, 0))
    new_y = coef_keep * efield[1] + coef_curl * (change(0, 0) - change(2, 1))
    new_z = coef_keep * efield[2] + coef_curl * (change(1, 1) - change(0, 2))
    return (new_x, new_y, new_z)

def spectrum(extent, orders, offset, period):
    cell_ids = jnp.arange(extent, dtype=jnp.int32) + offset
    order_ids = jnp.arange(orders, dtype=jnp.int32) - orders // 2
    wrapped = order_ids[:, None] * cell_ids[None, :] % period
    angles = 2.0 * math.pi / period * wrapped.astype(jnp.float32)
    return (jnp.cos(angles), jnp.sin(angles))

def image_tables(pixels, orders_p, orders_q):
    cos_u, sin_u = spectrum(pixels, orders_p, 0, pixels)
    row_table = (jnp.concatenate((cos_u.T, sin_u.T), 1) * (1.0 / math.sqrt(orders_p))).astype(jnp.bfloat16)
    cos_v, sin_v = spectrum(pixels, orders_q, 0, pixels)
    real_v = (cos_v * (1.0 / math.sqrt(orders_q))).astype(jnp.bfloat16)
    imag_v = (sin_v * (1.0 / math.sqrt(orders_q))).astype(jnp.bfloat16)
    g_matrix = jnp.concatenate((jnp.concatenate((real_v, imag_v), 1), jnp.concatenate((-imag_v, real_v), 1)), 0)
    return (row_table, g_matrix)

def source_columns(masked, g_matrix, pixels):
    halves = jnp.concatenate((jnp.concatenate((masked[0, 0], masked[1, 0]), 1), jnp.concatenate((masked[0, 1], masked[1, 1]), 1)), 0)
    spread = jnp.dot(halves, g_matrix, preferred_element_type=jnp.float32).astype(jnp.bfloat16)
    count_p = masked.shape[2]
    real_x = spread[:count_p, :pixels]
    imag_x = spread[:count_p, pixels:]
    real_y = spread[count_p:, :pixels]
    imag_y = spread[count_p:, pixels:]
    upper = jnp.concatenate((real_x, imag_x, real_y, imag_y), 1)
    lower = jnp.concatenate((-imag_x, real_x, -imag_y, real_y), 1)
    return jnp.concatenate((upper, lower), 0)

def reference(fields, material_map, material_eps, material_loss, source_shift, source_mask, source_weight):
    keep_table = (1.0 - material_loss) / (1.0 + material_loss)
    curl_table = COURANT / (material_eps * (1.0 + material_loss))
    coef_keep = keep_table[material_map]
    coef_curl = curl_table[material_map]
    middle = fields.shape[1] // 2
    efield = (fields[0], fields[1], fields[2])
    hfield = (fields[3], fields[4], fields[5])
    zeros_plane = jnp.zeros((2, fields.shape[2], fields.shape[3]), jnp.float32)

    def advance(turn_index, state_now):
        efield, hfield, phase_re, phase_im = state_now
        hfield = magnetic(efield, hfield, {})
        efield = electric(efield, hfield, coef_keep, coef_curl, {})
        moment = jnp.float32(ANGULAR) * (turn_index + 1).astype(jnp.float32)
        monitor = jnp.stack((efield[0][middle], efield[1][middle]))
        phase_re = phase_re + monitor * jnp.cos(moment)
        phase_im = phase_im - monitor * jnp.sin(moment)
        return (efield, hfield, phase_re, phase_im)
    efield, hfield, phase_re, phase_im = lax.fori_loop(0, STEPS, advance, (efield, hfield, zeros_plane, zeros_plane))
    final_fields = jnp.stack(efield + hfield)
    cos_x, sin_x = spectrum(NX, P_SIZE, 0, NX)
    cos_y, sin_y = spectrum(NY, Q, 0, NY)
    part_re = jnp.einsum('cxy,qy->cxq', phase_re, cos_y, precision=PRECISE) + jnp.einsum('cxy,qy->cxq', phase_im, sin_y, precision=PRECISE)
    part_im = jnp.einsum('cxy,qy->cxq', phase_im, cos_y, precision=PRECISE) - jnp.einsum('cxy,qy->cxq', phase_re, sin_y, precision=PRECISE)
    order_re = jnp.einsum('px,cxq->cpq', cos_x, part_re, precision=PRECISE) + jnp.einsum('px,cxq->cpq', sin_x, part_im, precision=PRECISE)
    order_im = jnp.einsum('px,cxq->cpq', cos_x, part_im, precision=PRECISE) - jnp.einsum('px,cxq->cpq', sin_x, part_re, precision=PRECISE)
    scaling = 1.0 / math.sqrt(NX * NY * STEPS)
    orders_b = (jnp.stack((order_re, order_im)) * scaling).astype(jnp.bfloat16)
    row_table, g_matrix = image_tables(M, P_SIZE, Q)

    def add_source(running, inputs):
        offsets, passed, weight = inputs
        rolled = jnp.roll(orders_b, (-offsets[0], -offsets[1]), axis=(2, 3))
        masked = rolled * passed.astype(jnp.bfloat16)
        columns = source_columns(masked, g_matrix, M)
        fields_img = jnp.dot(row_table, columns, preferred_element_type=jnp.float32)
        squared = fields_img * fields_img
        bright = squared.reshape(M, 4, M).sum(axis=1)
        return (running + weight / SOURCES * bright, None)
    image, unused = lax.scan(add_source, jnp.zeros((M, M), jnp.float32), (source_shift, source_mask, source_weight))
    return (final_fields, image)
```

```python
import functools
import math

import jax
import jax.numpy as jnp
import numpy as np
from jax import lax
from jax.experimental import pallas as pl
from jax.experimental.pallas import tpu as pltpu
from jax.sharding import PartitionSpec as P

STEPS = 12
ROUNDS = 2
M = 512
REACH = 8

COURANT = 0.55
ANGULAR = 0.7
PRECISE = lax.Precision.HIGHEST


F32 = jnp.float32
BF16 = jnp.bfloat16


def vmem():
    return pl.BlockSpec(memory_space=pltpu.VMEM)


def smem():
    return pl.BlockSpec(memory_space=pltpu.SMEM)


def call(kernel, ins, outs, scratch=(), name=None):
    spaces = {"v": vmem, "s": smem}
    return pl.pallas_call(
        kernel,
        out_shape=outs,
        in_specs=[spaces[space]() for _, space in ins],
        out_specs=[vmem() for _ in outs],
        scratch_shapes=list(scratch),
        name=name,
    )(*[array for array, _ in ins])


def shape(*dims, dtype=F32):
    return jax.ShapeDtypeStruct(dims, dtype)


def swap(values, axis, first):
    count = lax.axis_size(axis)
    pairs = []
    for low in range(first, count - 1, 2):
        pairs += [(low, low + 1), (low + 1, low)]
    if not pairs:
        return jnp.zeros_like(values)
    return lax.ppermute(values, axis, pairs)


def cyclic(values, axis, by):
    count = lax.axis_size(axis)
    return lax.ppermute(values, axis, [(i, (i + by) % count) for i in range(count)])


def waves(order_ids, cell_ids, period):
    wrapped = (order_ids[:, None] * cell_ids[None, :]) % period
    angles = 2.0 * math.pi / period * wrapped
    return np.cos(angles), np.sin(angles)


def pack_kernel(
    fields, materials, shifts, weights, masks, send_a, send_b, send_c, send_d, source_pack, rows, *, geo
):
    depth, cells_x, lanes, halo, slot = geo
    even_x = lax.axis_index("gx") % 2 == 0
    even_y = lax.axis_index("gy") % 2 == 0
    lane = lax.broadcasted_iota(jnp.int32, (depth, lanes), 1)
    for comp in range(7):
        high = jnp.zeros((depth, lanes), F32)
        low = jnp.zeros((depth, lanes), F32)
        for x in range(cells_x):
            if comp < 6:
                values = fields[comp, pl.ds(x, depth, stride=cells_x), :]
            else:
                values = materials[pl.ds(x, depth, stride=cells_x), :].astype(F32)
            rows[x, comp] = values
            here = (lane >= slot * x) & (lane < slot * (x + 1))
            high = jnp.where(here, pltpu.roll(values, (slot * x + slot) % lanes, 1), high)
            low = jnp.where(here, pltpu.roll(values, slot * x, 1) if x else values, low)
        send_c[comp] = jnp.where(even_y, high, low)
        send_d[comp] = jnp.where(even_y, low, high)
    far = cells_x - halo
    send_a[...] = rows[pl.ds(jnp.where(even_x, far, 0), halo)]
    send_b[...] = rows[pl.ds(jnp.where(even_x, 0, far), halo)]
    orders_p, orders_q = masks.shape[1:]
    source_pack[...] = jnp.zeros(source_pack.shape, F32)
    for source in range(masks.shape[0]):
        source_pack[source, 0:orders_p, 0:orders_q] = masks[source].astype(F32)
        spot = lax.broadcasted_iota(jnp.int32, (8, source_pack.shape[2]), 1)
        facts = jnp.where(spot == 0, shifts[source, 0].astype(F32), 0.0)
        facts = jnp.where(spot == 1, shifts[source, 1].astype(F32), facts)
        facts = jnp.where(spot == 2, weights[source], facts)
        source_pack[source, orders_p : orders_p + 8, :] = facts


def inside_lanes(lane, cells_y, total_y, slot):
    start = lax.axis_index("gy") * cells_y
    ring = 2 * cells_y
    place = start + jnp.where(lane < cells_y + slot, lane, lane - ring)
    held = (lane < cells_y + slot) | (lane >= ring - slot)
    return held & (place >= 0) & (place < total_y)


def run_steps(state, keep, curl, gate, phase, moments, first_step, geo, count):
    depth, cells_x, lanes, halo, slot = geo
    ring = 2 * lanes
    middle = depth // 2
    level = lax.broadcasted_iota(jnp.int32, (depth, ring), 0)
    at_top = level == depth - 1
    at_bottom = level == 0

    def next_y(values):
        return pltpu.roll(values, ring - 1, 1)

    def last_y(values):
        return pltpu.roll(values, 1, 1)

    def next_z(values):
        return jnp.where(at_top, 0.0, pltpu.roll(values, depth - 1, 0))

    def last_z(values):
        return jnp.where(at_bottom, 0.0, pltpu.roll(values, 1, 0))

    def step(index, carry):
        def row(i, inner):
            ex, ey, ez = state[0, i], state[1, i], state[2, i]
            open_h = gate[i]
            hx = state[3, i] - open_h * ((next_y(ez) - ez) - (next_z(ey) - ey))
            hy = state[4, i] - open_h * ((next_z(ex) - ex) - (state[2, i + 1] - ez))
            hz = state[5, i] - open_h * ((state[1, i + 1] - ey) - (next_y(ex) - ex))
            state[3, i] = hx
            state[4, i] = hy
            state[5, i] = hz
            before = jnp.maximum(i - 1, 0)
            kept, turned = keep[i], curl[i]
            state[0, i] = kept * ex + turned * ((hz - last_y(hz)) - (hy - last_z(hy)))
            state[1, i] = kept * ey + turned * ((hx - last_z(hx)) - (hz - state[5, before]))
            state[2, i] = kept * ez + turned * ((hy - state[4, before]) - (hx - last_y(hx)))
            return inner

        lax.fori_loop(index, cells_x + 2 * halo - 1 - index, row, 0)
        at = first_step + index
        cosine, sine = moments[at, 0], moments[at, 1]
        for comp in range(2):
            monitor = state[comp, halo : halo + cells_x, middle, 0:lanes]
            low = comp * cells_x
            phase[low : low + cells_x, :] = phase[low : low + cells_x, :] + monitor * cosine
            low = (2 + comp) * cells_x
            phase[low : low + cells_x, :] = phase[low : low + cells_x, :] - monitor * sine
        return carry

    lax.fori_loop(0, count, step, 0)


def set_gate(gate, geo, total_x, total_y):
    depth, cells_x, lanes, halo, slot = geo
    lane = lax.broadcasted_iota(jnp.int32, (1, 2 * lanes), 1)
    held = jnp.where(inside_lanes(lane, lanes, total_y, slot), COURANT, 0.0).astype(F32)
    start = lax.axis_index("gx") * cells_x - halo
    for i in range(cells_x + 2 * halo):
        place = start + i
        gate[i] = jnp.where((place >= 0) & (place < total_x), held, 0.0)


def first_kernel(
    fields, materials, got_a, got_b, got_c, got_d, edge_a, edge_b, tables, moments,
    own, keep, curl, phase, send_a, send_b,
    state, gate, *, geo, total_x, total_y, count,
):
    depth, cells_x, lanes, halo, slot = geo
    odd_x = lax.axis_index("gx") % 2 == 1
    even_y = lax.axis_index("gy") % 2 == 0
    lane = lax.broadcasted_iota(jnp.int32, (depth, lanes), 1)
    all_lane = lax.broadcasted_iota(jnp.int32, (1, 2 * lanes), 1)
    inside_y = inside_lanes(all_lane, lanes, total_y, slot)
    start_x = lax.axis_index("gx") * cells_x - halo
    set_gate(gate, geo, total_x, total_y)

    def side(left, right, row):
        right = pltpu.roll(right, (-slot * row) % lanes, 1)
        left = pltpu.roll(left, (lanes - slot - slot * row) % lanes, 1)
        return jnp.where(lane < slot, right, jnp.where(lane >= lanes - slot, left, 0.0))

    def place(comp, i, main, more):
        if comp < 6:
            state[comp, i, :, 0:lanes] = main
            state[comp, i, :, lanes : 2 * lanes] = more
            return
        kind = jnp.concatenate((main, more), 1)
        row_in = (start_x + i >= 0) & (start_x + i < total_x)
        kept = jnp.zeros(kind.shape, F32)
        turned = jnp.zeros(kind.shape, F32)
        here = inside_y & row_in
        for material in range(tables.shape[1]):
            match = (kind == float(material)) & here
            kept = jnp.where(match, tables[0, material], kept)
            turned = jnp.where(match, tables[1, material], turned)
        keep[i] = kept
        curl[i] = turned

    base_a = jnp.where(odd_x, 0, cells_x + halo)
    base_b = jnp.where(odd_x, cells_x + halo, 0)
    from_a = jnp.where(odd_x, cells_x - halo, 0)
    from_b = jnp.where(odd_x, 0, cells_x - halo)
    for comp in range(7):
        c_pack, d_pack = got_c[comp], got_d[comp]
        left = jnp.where(even_y, d_pack, c_pack)
        right = jnp.where(even_y, c_pack, d_pack)
        for x in range(cells_x):
            if comp < 6:
                main = fields[comp, pl.ds(x, depth, stride=cells_x), :]
            else:
                main = materials[pl.ds(x, depth, stride=cells_x), :].astype(F32)
            place(comp, halo + x, main, side(left, right, x))
        for got, edge, base, origin in (
            (got_a, edge_a, base_a, from_a),
            (got_b, edge_b, base_b, from_b),
        ):
            c_pack, d_pack = edge[0, comp], edge[1, comp]
            left = jnp.where(even_y, d_pack, c_pack)
            right = jnp.where(even_y, c_pack, d_pack)
            for r in range(halo):
                place(comp, base + r, got[r, comp], side(left, right, origin + r))

    phase[...] = jnp.zeros(phase.shape, F32)
    run_steps(state, keep, curl, gate, phase, moments, 0, geo, count)

    for comp in range(6):
        own[comp] = state[comp, halo : halo + cells_x]
    width = lanes // cells_x
    for send, first in ((send_a, base_b), (send_b, base_a)):
        origin = jnp.where(first == 0, cells_x, halo)
        for comp in range(6):
            edges = jnp.zeros((depth, lanes), F32)
            for r in range(halo):
                send[r, comp] = state[comp, origin + r, :, 0:lanes]
                more = state[comp, origin + r, :, lanes : 2 * lanes]
                here = (lane >= width * r) & (lane < width * (r + 1))
                edges = jnp.where(here, pltpu.roll(more, (width * r + width // 2) % lanes, 1), edges)
            send[halo, comp] = edges


def second_kernel(
    own, keep, curl, phase_in, got_a, got_b, moments,
    final, phase,
    state, gate, *, geo, total_x, total_y, count,
):
    depth, cells_x, lanes, halo, slot = geo
    odd_x = lax.axis_index("gx") % 2 == 1
    lane = lax.broadcasted_iota(jnp.int32, (depth, lanes), 1)
    set_gate(gate, geo, total_x, total_y)
    base_a = jnp.where(odd_x, 0, cells_x + halo)
    base_b = jnp.where(odd_x, cells_x + halo, 0)
    width = lanes // cells_x
    half = width // 2
    edge = (lane < half) | (lane >= lanes - half)
    for comp in range(6):
        state[comp, halo : halo + cells_x] = own[comp]
        for got, base in ((got_a, base_a), (got_b, base_b)):
            pack = got[halo, comp]
            for r in range(halo):
                state[comp, base + r, :, 0:lanes] = got[r, comp]
                more = pltpu.roll(pack, (-(width * r + half)) % lanes, 1)
                state[comp, base + r, :, lanes : 2 * lanes] = jnp.where(edge, more, 0.0)
    phase[...] = phase_in[...]
    run_steps(state, keep, curl, gate, phase, moments, count, geo, count)
    for comp in range(6):
        for x in range(cells_x):
            final[comp, pl.ds(x, depth, stride=cells_x), :] = state[comp, halo + x, :, 0:lanes]


def along_y_kernel(*refs, count):
    pieces, table, part = refs[:count], refs[count], refs[count + 1]
    me = lax.axis_index("gy")
    total = None
    for back, piece in enumerate(pieces):
        origin = (me - back + count) % count
        term = jnp.dot(piece[...], table[origin], precision=PRECISE, preferred_element_type=F32)
        total = term if total is None else total + term
    rows, width = total.shape[0] // 2, total.shape[1] // 2
    re_cos, re_sin = total[:rows, :width], total[:rows, width:]
    im_cos, im_sin = total[rows:, :width], total[rows:, width:]
    part[:, 0:width] = re_cos + im_sin
    part[:, width : 2 * width] = im_cos - re_sin


def image_kernel(*refs, tiles_x, tiles_y, cells_x, scaling, sources_all):
    parts, refs = refs[:tiles_x], refs[tiles_x:]
    packs, refs = refs[:tiles_y], refs[tiles_y:]
    table_x, g_matrix, row_table, shifts, weights = refs[:5]
    strips, refs = refs[5 : 5 + tiles_x], refs[5 + tiles_x :]
    gathered, orders, columns, rows, total = refs
    me_x = lax.axis_index("gx")
    me_y = lax.axis_index("gy")
    width = orders.shape[2]
    reach = orders.shape[1]
    for back, part in enumerate(parts):
        origin = pl.multiple_of((me_x - back + tiles_x) % tiles_x * cells_x, cells_x)
        for comp in range(2):
            gathered[comp, pl.ds(origin, cells_x), :] = part[comp * cells_x : (comp + 1) * cells_x, :]
    for comp in range(2):
        re, im = gathered[comp, :, 0:width], gathered[comp, :, width : 2 * width]
        dot = functools.partial(jnp.dot, precision=PRECISE, preferred_element_type=F32)
        cos_x, sin_x = table_x[0:reach, :], table_x[reach : 2 * reach, :]
        order_re = dot(cos_x, re) + dot(sin_x, im)
        order_im = dot(cos_x, im) - dot(sin_x, re)
        orders[2 * comp] = (order_re * scaling).astype(BF16).astype(F32)
        orders[2 * comp + 1] = (order_im * scaling).astype(BF16).astype(F32)
    strip = row_table.shape[1]
    for ahead in range(tiles_x):
        owner = (me_x + ahead) % tiles_x * tiles_y + me_y
        rows[strip * ahead : strip * (ahead + 1), :] = row_table[owner]
    pixels = g_matrix.shape[1] // 2
    orders_p = rows.shape[1] // 2
    local = packs[0].shape[0]
    total[...] = jnp.zeros(total.shape, F32)
    for at, pack in enumerate(packs):

        def source(index, carry, at=at, pack=pack):
            number = at * local + index
            down = shifts[number, 0] + REACH
            across = width - (shifts[number, 1] + REACH)
            passed = pack[index, 0:orders_p, :]
            masked = []
            for plane in range(4):
                window = orders[plane, pl.ds(down, orders_p), :]
                masked.append((pltpu.roll(window, across, 1) * passed).astype(BF16))
            halves = jnp.concatenate(
                (jnp.concatenate(masked[:2], 1), jnp.concatenate(masked[2:], 1)), 0
            )
            spread = jnp.dot(halves, g_matrix[...], preferred_element_type=F32).astype(BF16)
            for comp in range(2):
                part = spread[comp * orders_p : (comp + 1) * orders_p]
                real, imag = part[:, :pixels], part[:, pixels:]
                low = 2 * comp * pixels
                columns[0:orders_p, low : low + pixels] = real
                columns[0:orders_p, low + pixels : low + 2 * pixels] = imag
                columns[orders_p : 2 * orders_p, low : low + pixels] = -imag
                columns[orders_p : 2 * orders_p, low + pixels : low + 2 * pixels] = real
            bright = None
            for block in range(4):
                value = jnp.dot(
                    rows[...],
                    columns[:, block * pixels : (block + 1) * pixels],
                    preferred_element_type=F32,
                )
                bright = value * value if bright is None else bright + value * value
            total[...] = total[...] + (weights[number] / sources_all) * bright
            return carry

        lax.fori_loop(0, local, source, 0)
    for ahead in range(tiles_x):
        strips[ahead][...] = total[strip * ahead : strip * (ahead + 1), :]


def body(
    fields, material_map, material_eps, material_loss, source_shift, source_mask, source_weight
):
    tiles_x = lax.axis_size("gx")
    tiles_y = lax.axis_size("gy")
    _, depth, cells_x, lanes = fields.shape
    total_x, total_y = cells_x * tiles_x, lanes * tiles_y
    count = STEPS // ROUNDS
    halo = count
    slot = lanes // cells_x
    assert halo <= cells_x and slot >= STEPS and slot // 2 >= halo
    geo = (depth, cells_x, lanes, halo, slot)
    flat_fields = fields.reshape(6, depth * cells_x, lanes)
    flat_map = material_map.reshape(depth * cells_x, lanes)
    local, orders_p, orders_q = source_mask.shape
    wide = 128

    keep_table = (1.0 - material_loss) / (1.0 + material_loss)
    curl_table = COURANT / (material_eps * (1.0 + material_loss))
    tables = jnp.stack((keep_table, curl_table))
    angle = np.float32(ANGULAR) * np.arange(1, STEPS + 1, dtype=np.float32)
    moments = jnp.asarray(np.stack((np.cos(angle), np.sin(angle)), 1).astype(np.float32))

    row_shape = shape(halo, 7, depth, lanes)
    edge_shape = shape(7, depth, lanes)
    to_a, to_b, to_c, to_d, my_pack = call(
        functools.partial(pack_kernel, geo=geo),
        [(flat_fields, "v"), (flat_map, "v"), (source_shift, "s"), (source_weight, "s"), (source_mask, "v")],
        [row_shape, row_shape, edge_shape, edge_shape, shape(local, orders_p + 8, wide)],
        [pltpu.VMEM((cells_x, 7, depth, lanes), F32)],
        name="pack",
    )
    got_c = swap(to_c, "gy", 0)
    got_d = swap(to_d, "gy", 1)
    got_a = swap(to_a, "gx", 0)
    got_b = swap(to_b, "gx", 1)
    edges = jnp.stack((got_c, got_d))
    edge_a = swap(edges, "gx", 0)
    edge_b = swap(edges, "gx", 1)
    packs = [my_pack] + [cyclic(my_pack, "gy", by) for by in range(1, tiles_y)]

    span = cells_x + 2 * halo
    state = pltpu.VMEM((6, span, depth, 2 * lanes), F32)
    gate = pltpu.VMEM((span, 1, 2 * lanes), F32)
    coef_shape = shape(span, depth, 2 * lanes)
    phase_shape = shape(4 * cells_x, lanes)
    send_shape = shape(halo + 1, 6, depth, lanes)
    own, keep, curl, phase, to_a, to_b = call(
        functools.partial(first_kernel, geo=geo, total_x=total_x, total_y=total_y, count=count),
        [(flat_fields, "v"), (flat_map, "v"), (got_a, "v"), (got_b, "v"), (got_c, "v"), (got_d, "v"),
         (edge_a, "v"), (edge_b, "v"), (tables, "s"), (moments, "s")],
        [shape(6, cells_x, depth, 2 * lanes), coef_shape, coef_shape, phase_shape, send_shape, send_shape],
        [state, gate],
        name="steps_first",
    )
    got_a = swap(to_a, "gx", 0)
    got_b = swap(to_b, "gx", 1)
    final, phase = call(
        functools.partial(second_kernel, geo=geo, total_x=total_x, total_y=total_y, count=count),
        [(own, "v"), (keep, "v"), (curl, "v"), (phase, "v"), (got_a, "v"), (got_b, "v"), (moments, "s")],
        [shape(6, depth * cells_x, lanes), phase_shape],
        [state, gate],
        name="steps_second",
    )
    final_fields = final.reshape(fields.shape)

    reach = orders_p + 2 * REACH
    ids_p = np.arange(-REACH, orders_p + REACH) % orders_p - orders_p // 2
    ids_q = np.arange(-REACH, orders_q + REACH) % orders_q - orders_q // 2
    cos_y, sin_y = waves(ids_q, np.arange(total_y), total_y)
    table_y = np.zeros((total_y, 2 * wide), np.float32)
    table_y[:, : len(ids_q)] = cos_y.T
    table_y[:, wide : wide + len(ids_q)] = sin_y.T
    cos_x, sin_x = waves(ids_p, np.arange(total_x), total_x)
    table_x = np.concatenate((cos_x, sin_x), 0).astype(np.float32)
    pixels = M
    cos_u, sin_u = waves(np.arange(orders_p) - orders_p // 2, np.arange(pixels), pixels)
    strip = pixels // (tiles_x * tiles_y)
    row_table = (np.concatenate((cos_u, sin_u), 0).T / math.sqrt(orders_p)).astype(np.float32)
    row_table = row_table.reshape(tiles_x * tiles_y, strip, 2 * orders_p).astype(jnp.bfloat16)
    cos_v, sin_v = waves(np.arange(orders_q) - orders_q // 2, np.arange(pixels), pixels)
    g_matrix = np.zeros((2 * wide, 2 * pixels), np.float32)
    g_matrix[:orders_q, :pixels] = cos_v / math.sqrt(orders_q)
    g_matrix[:orders_q, pixels:] = sin_v / math.sqrt(orders_q)
    g_matrix[wide : wide + orders_q, :pixels] = -sin_v / math.sqrt(orders_q)
    g_matrix[wide : wide + orders_q, pixels:] = cos_v / math.sqrt(orders_q)
    g_matrix = g_matrix.astype(jnp.bfloat16)

    pieces = [phase] + [cyclic(phase, "gy", by) for by in range(1, tiles_y)]
    (part,) = call(
        functools.partial(along_y_kernel, count=tiles_y),
        [(piece, "v") for piece in pieces]
        + [(jnp.asarray(table_y.reshape(tiles_y, lanes, 2 * wide)), "v")],
        [shape(2 * cells_x, 2 * wide)],
        name="along_y",
    )
    parts = [part] + [cyclic(part, "gx", by) for by in range(1, tiles_x)]

    facts = jnp.concatenate([pack[:, orders_p, 0:3] for pack in packs], 0)
    shifts = facts[:, 0:2].astype(jnp.int32)
    weights = facts[:, 2]
    strips = call(
        functools.partial(
            image_kernel,
            tiles_x=tiles_x,
            tiles_y=tiles_y,
            cells_x=cells_x,
            scaling=1.0 / math.sqrt(total_x * total_y * STEPS),
            sources_all=local * tiles_x * tiles_y,
        ),
        [(piece, "v") for piece in parts]
        + [(pack, "v") for pack in packs]
        + [(jnp.asarray(table_x), "v"), (jnp.asarray(g_matrix), "v"), (jnp.asarray(row_table), "v"),
           (shifts, "s"), (weights, "s")],
        [shape(strip, pixels) for _ in range(tiles_x)],
        [
            pltpu.VMEM((2, total_x, 2 * wide), F32),
            pltpu.VMEM((4, reach, wide), F32),
            pltpu.VMEM((2 * orders_p, 4 * pixels), BF16),
            pltpu.VMEM((tiles_x * strip, 2 * orders_p), BF16),
            pltpu.VMEM((tiles_x * strip, pixels), F32),
        ],
        name="image",
    )
    image = strips[0]
    for by in range(1, tiles_x):
        image = image + cyclic(strips[by], "gx", by)
    return (final_fields, image)


def solution(mesh):
    placed = (
        P("clips", None, "gx", "gy"),
        P("clips", "gx", "gy"),
        P(),
        P(),
        P(("gx", "gy"), None),
        P(("gx", "gy"), None, None),
        P(("gx", "gy")),
    )
    return jax.shard_map(
        body,
        mesh=mesh,
        in_specs=placed,
        out_specs=(P("clips", None, "gx", "gy"), P(("gx", "gy"), "clips")),
        check_vma=False,
    )
```

```python
import functools
import math

import jax
import jax.numpy as jnp
import numpy as np
from jax import lax
from jax.experimental import pallas as pl
from jax.experimental.pallas import tpu as pltpu
from jax.sharding import PartitionSpec as P

STEPS = 12
ROUNDS = 2
M = 512
REACH = 8

COURANT = 0.55
ANGULAR = 0.7
PRECISE = lax.Precision.HIGHEST


F32 = jnp.float32
BF16 = jnp.bfloat16


def vmem():
    return pl.BlockSpec(memory_space=pltpu.VMEM)


def smem():
    return pl.BlockSpec(memory_space=pltpu.SMEM)


def call(kernel, ins, outs, scratch=(), limit=16):
    spaces = {"h": vmem, "v": vmem, "s": smem}

    def out_spec(out):
        return vmem() if not isinstance(out, jax.ShapeDtypeStruct) else pl.BlockSpec(memory_space=pl.ANY)

    held = [
        pltpu.with_memory_space_constraint(array, pltpu.VMEM) if space == "v" else array
        for array, space in ins
    ]
    return pl.pallas_call(
        kernel,
        out_shape=outs,
        in_specs=[spaces[space]() for _, space in ins],
        out_specs=[out_spec(out) for out in outs],
        scratch_shapes=list(scratch),
        compiler_params=pltpu.CompilerParams(vmem_limit_bytes=limit << 20),
    )(*held)


def shape(*dims, dtype=F32):
    return pltpu.VMEM(dims, dtype)


def swap(values, axis, first):
    count = lax.axis_size(axis)
    pairs = []
    for low in range(first, count - 1, 2):
        pairs += [(low, low + 1), (low + 1, low)]
    if not pairs:
        return jnp.zeros_like(values)
    return lax.ppermute(values, axis, pairs)


def cyclic(values, axis, by):
    count = lax.axis_size(axis)
    return lax.ppermute(values, axis, [(i, (i + by) % count) for i in range(count)])


def waves(order_ids, cell_ids, period):
    wrapped = (order_ids[:, None] * cell_ids[None, :]) % period
    angles = 2.0 * math.pi / period * wrapped
    return np.cos(angles), np.sin(angles)


def pack_kernel(
    fields, materials, shifts, weights, masks, send_a, send_b, send_c, send_d, source_pack, rows, *, geo
):
    depth, cells_x, lanes, halo, slot = geo
    even_x = lax.axis_index("gx") % 2 == 0
    even_y = lax.axis_index("gy") % 2 == 0
    lane = lax.broadcasted_iota(jnp.int32, (depth, lanes), 1)
    for comp in range(7):
        high = jnp.zeros((depth, lanes), F32)
        low = jnp.zeros((depth, lanes), F32)
        for x in range(cells_x):
            if comp < 6:
                values = fields[comp, pl.ds(x, depth, stride=cells_x), :]
            else:
                values = materials[pl.ds(x, depth, stride=cells_x), :].astype(F32)
            rows[x, comp] = values
            here = (lane >= slot * x) & (lane < slot * (x + 1))
            high = jnp.where(here, pltpu.roll(values, (slot * x + slot) % lanes, 1), high)
            low = jnp.where(here, pltpu.roll(values, slot * x, 1) if x else values, low)
        send_c[comp] = jnp.where(even_y, high, low)
        send_d[comp] = jnp.where(even_y, low, high)
    far = cells_x - halo
    send_a[...] = rows[pl.ds(jnp.where(even_x, far, 0), halo)]
    send_b[...] = rows[pl.ds(jnp.where(even_x, 0, far), halo)]
    orders_p, orders_q = masks.shape[1:]
    source_pack[...] = jnp.zeros(source_pack.shape, F32)
    for source in range(masks.shape[0]):
        source_pack[source, 0:orders_p, 0:orders_q] = masks[source].astype(F32)
        for at, fact in enumerate((shifts[0, source], shifts[1, source], weights[source])):
            source_pack[source, orders_p : orders_p + 1, at : at + 1] = jnp.full((1, 1), fact).astype(F32)


def inside_lanes(lane, cells_y, total_y, slot):
    start = lax.axis_index("gy") * cells_y
    ring = 2 * cells_y
    place = start + jnp.where(lane < cells_y + slot, lane, lane - ring)
    held = (lane < cells_y + slot) | (lane >= ring - slot)
    return held & (place >= 0) & (place < total_y)


def run_steps(state, keep, curl, gate, phase, moments, first_step, geo, count):
    depth, cells_x, lanes, halo, _ = geo
    ring = 2 * lanes
    middle = depth // 2
    level = lax.broadcasted_iota(jnp.int32, (depth, ring), 0)
    at_top = level == depth - 1
    at_bottom = level == 0

    def next_y(values):
        return pltpu.roll(values, ring - 1, 1)

    def last_y(values):
        return pltpu.roll(values, 1, 1)

    def next_z(values):
        return jnp.where(at_top, 0.0, pltpu.roll(values, depth - 1, 0))

    def last_z(values):
        return jnp.where(at_bottom, 0.0, pltpu.roll(values, 1, 0))

    def step(index, carry):
        def row(i, inner):
            ex, ey, ez = state[0, i], state[1, i], state[2, i]
            open_h = gate[i]
            hx = state[3, i] - open_h * ((next_y(ez) - ez) - (next_z(ey) - ey))
            hy = state[4, i] - open_h * ((next_z(ex) - ex) - (state[2, i + 1] - ez))
            hz = state[5, i] - open_h * ((state[1, i + 1] - ey) - (next_y(ex) - ex))
            state[3, i] = hx
            state[4, i] = hy
            state[5, i] = hz
            before = jnp.maximum(i - 1, 0)
            kept, turned = keep[i], curl[i]
            state[0, i] = kept * ex + turned * ((hz - last_y(hz)) - (hy - last_z(hy)))
            state[1, i] = kept * ey + turned * ((hx - last_z(hx)) - (hz - state[5, before]))
            state[2, i] = kept * ez + turned * ((hy - state[4, before]) - (hx - last_y(hx)))
            return inner

        lax.fori_loop(index, cells_x + 2 * halo - 1 - index, row, 0)
        at = first_step + index
        cosine, sine = moments[at, 0], moments[at, 1]
        for comp in range(2):
            monitor = state[comp, halo : halo + cells_x, middle, 0:lanes]
            low = comp * cells_x
            phase[low : low + cells_x, :] = phase[low : low + cells_x, :] + monitor * cosine
            low = (2 + comp) * cells_x
            phase[low : low + cells_x, :] = phase[low : low + cells_x, :] - monitor * sine
        return carry

    lax.fori_loop(0, count, step, 0)


def set_gate(gate, geo, total_x, total_y):
    _, cells_x, lanes, halo, slot = geo
    lane = lax.broadcasted_iota(jnp.int32, (1, 2 * lanes), 1)
    held = jnp.where(inside_lanes(lane, lanes, total_y, slot), COURANT, 0.0).astype(F32)
    start = lax.axis_index("gx") * cells_x - halo
    for i in range(cells_x + 2 * halo):
        place = start + i
        gate[i] = jnp.where((place >= 0) & (place < total_x), held, 0.0)


def first_kernel(
    fields, materials, got_a, got_b, got_c, got_d, edge_a, edge_b, tables, moments,
    own, keep, curl, phase, send_a, send_b,
    state, gate, *, geo, total_x, total_y, count,
):
    depth, cells_x, lanes, halo, slot = geo
    odd_x = lax.axis_index("gx") % 2 == 1
    even_y = lax.axis_index("gy") % 2 == 0
    lane = lax.broadcasted_iota(jnp.int32, (depth, lanes), 1)
    all_lane = lax.broadcasted_iota(jnp.int32, (1, 2 * lanes), 1)
    inside_y = inside_lanes(all_lane, lanes, total_y, slot)
    start_x = lax.axis_index("gx") * cells_x - halo
    set_gate(gate, geo, total_x, total_y)

    def side(left, right, row):
        right = pltpu.roll(right, (-slot * row) % lanes, 1)
        left = pltpu.roll(left, (lanes - slot - slot * row) % lanes, 1)
        return jnp.where(lane < slot, right, jnp.where(lane >= lanes - slot, left, 0.0))

    def place(comp, i, main, more):
        if comp < 6:
            state[comp, i, :, 0:lanes] = main
            state[comp, i, :, lanes : 2 * lanes] = more
            return
        kind = jnp.concatenate((main, more), 1)
        row_in = (start_x + i >= 0) & (start_x + i < total_x)
        kept = jnp.zeros(kind.shape, F32)
        turned = jnp.zeros(kind.shape, F32)
        here = inside_y & row_in
        for material in range(tables.shape[1]):
            match = (kind == float(material)) & here
            kept = jnp.where(match, tables[0, material], kept)
            turned = jnp.where(match, tables[1, material], turned)
        keep[i] = kept
        curl[i] = turned

    base_a = jnp.where(odd_x, 0, cells_x + halo)
    base_b = jnp.where(odd_x, cells_x + halo, 0)
    from_a = jnp.where(odd_x, cells_x - halo, 0)
    from_b = jnp.where(odd_x, 0, cells_x - halo)
    for comp in range(7):
        c_pack, d_pack = got_c[comp], got_d[comp]
        left = jnp.where(even_y, d_pack, c_pack)
        right = jnp.where(even_y, c_pack, d_pack)
        for x in range(cells_x):
            if comp < 6:
                main = fields[comp, pl.ds(x, depth, stride=cells_x), :]
            else:
                main = materials[pl.ds(x, depth, stride=cells_x), :].astype(F32)
            place(comp, halo + x, main, side(left, right, x))
        for got, edge, base, origin in (
            (got_a, edge_a, base_a, from_a),
            (got_b, edge_b, base_b, from_b),
        ):
            c_pack, d_pack = edge[0, comp], edge[1, comp]
            left = jnp.where(even_y, d_pack, c_pack)
            right = jnp.where(even_y, c_pack, d_pack)
            for r in range(halo):
                place(comp, base + r, got[r, comp], side(left, right, origin + r))

    phase[...] = jnp.zeros(phase.shape, F32)
    run_steps(state, keep, curl, gate, phase, moments, 0, geo, count)

    for comp in range(6):
        own[comp] = state[comp, halo : halo + cells_x]
    width = lanes // cells_x
    for send, first in ((send_a, base_b), (send_b, base_a)):
        origin = jnp.where(first == 0, cells_x, halo)
        for comp in range(6):
            edges = jnp.zeros((depth, lanes), F32)
            for r in range(halo):
                send[r, comp] = state[comp, origin + r, :, 0:lanes]
                more = state[comp, origin + r, :, lanes : 2 * lanes]
                here = (lane >= width * r) & (lane < width * (r + 1))
                edges = jnp.where(here, pltpu.roll(more, (width * r + width // 2) % lanes, 1), edges)
            send[halo, comp] = edges


def second_kernel(
    own, keep, curl, phase_in, got_a, got_b, moments,
    final, phase,
    state, gate, *, geo, total_x, total_y, count,
):
    depth, cells_x, lanes, halo, _ = geo
    odd_x = lax.axis_index("gx") % 2 == 1
    lane = lax.broadcasted_iota(jnp.int32, (depth, lanes), 1)
    set_gate(gate, geo, total_x, total_y)
    base_a = jnp.where(odd_x, 0, cells_x + halo)
    base_b = jnp.where(odd_x, cells_x + halo, 0)
    width = lanes // cells_x
    half = width // 2
    edge = (lane < half) | (lane >= lanes - half)
    for comp in range(6):
        state[comp, halo : halo + cells_x] = own[comp]
        for got, base in ((got_a, base_a), (got_b, base_b)):
            pack = got[halo, comp]
            for r in range(halo):
                state[comp, base + r, :, 0:lanes] = got[r, comp]
                more = pltpu.roll(pack, (-(width * r + half)) % lanes, 1)
                state[comp, base + r, :, lanes : 2 * lanes] = jnp.where(edge, more, 0.0)
    phase[...] = phase_in[...]
    run_steps(state, keep, curl, gate, phase, moments, count, geo, count)
    for comp in range(6):
        for x in range(cells_x):
            final[comp, pl.ds(x, depth, stride=cells_x), :] = state[comp, halo + x, :, 0:lanes]


def along_y_kernel(*refs, count):
    pieces, (table, fields, part, kept, done) = refs[:count], refs[count:]
    keeping = pltpu.make_async_copy(fields, kept, done)
    keeping.start()
    me = lax.axis_index("gy")
    total = None
    for back, piece in enumerate(pieces):
        origin = (me - back + count) % count
        term = jnp.dot(piece[...], table[origin], precision=PRECISE, preferred_element_type=F32)
        total = term if total is None else total + term
    rows, width = total.shape[0] // 2, total.shape[1] // 2
    re_cos, re_sin = total[:rows, :width], total[:rows, width:]
    im_cos, im_sin = total[rows:, :width], total[rows:, width:]
    part[:, 0:width] = re_cos + im_sin
    part[:, width : 2 * width] = im_cos - re_sin
    keeping.wait()


def image_kernel(*refs, tiles_x, tiles_y, cells_x, scaling, sources_all):
    parts, refs = refs[:tiles_x], refs[tiles_x:]
    packs, refs = refs[:tiles_y], refs[tiles_y:]
    table_x, g_matrix, row_table, shifts, weights = refs[:5]
    strips, refs = refs[5 : 5 + tiles_x], refs[5 + tiles_x :]
    gathered, orders, columns, rows, total = refs
    me_x = lax.axis_index("gx")
    me_y = lax.axis_index("gy")
    width = orders.shape[2]
    reach = orders.shape[1]
    for back, part in enumerate(parts):
        origin = pl.multiple_of((me_x - back + tiles_x) % tiles_x * cells_x, cells_x)
        for comp in range(2):
            gathered[comp, pl.ds(origin, cells_x), :] = part[comp * cells_x : (comp + 1) * cells_x, :]
    for comp in range(2):
        re, im = gathered[comp, :, 0:width], gathered[comp, :, width : 2 * width]
        dot = functools.partial(jnp.dot, precision=PRECISE, preferred_element_type=F32)
        cos_x, sin_x = table_x[0:reach, :], table_x[reach : 2 * reach, :]
        order_re = dot(cos_x, re) + dot(sin_x, im)
        order_im = dot(cos_x, im) - dot(sin_x, re)
        orders[2 * comp] = (order_re * scaling).astype(BF16).astype(F32)
        orders[2 * comp + 1] = (order_im * scaling).astype(BF16).astype(F32)
    strip = row_table.shape[1]
    for ahead in range(tiles_x):
        owner = (me_x + ahead) % tiles_x * tiles_y + me_y
        rows[strip * ahead : strip * (ahead + 1), :] = row_table[owner]
    pixels = g_matrix.shape[1] // 2
    orders_p = rows.shape[1] // 2
    local = packs[0].shape[0]
    total[...] = jnp.zeros(total.shape, F32)
    for at, pack in enumerate(packs):

        def source(index, carry, at=at, pack=pack):
            number = at * local + index
            down = shifts[number, 0] + REACH
            across = width - (shifts[number, 1] + REACH)
            passed = pack[index, 0:orders_p, :]
            masked = []
            for plane in range(4):
                window = orders[plane, pl.ds(down, orders_p), :]
                masked.append((pltpu.roll(window, across, 1) * passed).astype(BF16))
            halves = jnp.concatenate(
                (jnp.concatenate(masked[:2], 1), jnp.concatenate(masked[2:], 1)), 0
            )
            spread = jnp.dot(halves, g_matrix[...], preferred_element_type=F32).astype(BF16)
            for comp in range(2):
                part = spread[comp * orders_p : (comp + 1) * orders_p]
                real, imag = part[:, :pixels], part[:, pixels:]
                low = 2 * comp * pixels
                columns[0:orders_p, low : low + pixels] = real
                columns[0:orders_p, low + pixels : low + 2 * pixels] = imag
                columns[orders_p : 2 * orders_p, low : low + pixels] = -imag
                columns[orders_p : 2 * orders_p, low + pixels : low + 2 * pixels] = real
            bright = None
            for block in range(4):
                value = jnp.dot(
                    rows[...],
                    columns[:, block * pixels : (block + 1) * pixels],
                    preferred_element_type=F32,
                )
                bright = value * value if bright is None else bright + value * value
            total[...] = total[...] + (weights[number] / sources_all) * bright
            return carry

        lax.fori_loop(0, local, source, 0)
    for ahead in range(tiles_x):
        strips[ahead][...] = total[strip * ahead : strip * (ahead + 1), :]


def body(
    fields, material_map, material_eps, material_loss, source_shift, source_mask, source_weight
):
    tiles_x = lax.axis_size("gx")
    tiles_y = lax.axis_size("gy")
    _, depth, cells_x, lanes = fields.shape
    total_x, total_y = cells_x * tiles_x, lanes * tiles_y
    count = STEPS // ROUNDS
    halo = count
    slot = lanes // cells_x
    assert halo <= cells_x and slot >= STEPS and slot // 2 >= halo
    geo = (depth, cells_x, lanes, halo, slot)
    flat_fields = fields.reshape(6, depth * cells_x, lanes)
    flat_map = material_map.reshape(depth * cells_x, lanes)
    local, orders_p, orders_q = source_mask.shape
    wide = 128

    keep_table = (1.0 - material_loss) / (1.0 + material_loss)
    curl_table = COURANT / (material_eps * (1.0 + material_loss))
    tables = jnp.stack((keep_table, curl_table))
    angle = np.float32(ANGULAR) * np.arange(1, STEPS + 1, dtype=np.float32)
    moments = jnp.asarray(np.stack((np.cos(angle), np.sin(angle)), 1).astype(np.float32))

    row_shape = shape(halo, 7, depth, lanes)
    edge_shape = shape(7, depth, lanes)
    to_a, to_b, to_c, to_d, my_pack = call(
        functools.partial(pack_kernel, geo=geo),
        [(flat_fields, "h"), (flat_map, "h"), (source_shift.T, "s"), (source_weight, "s"), (source_mask, "h")],
        [row_shape, row_shape, edge_shape, edge_shape, shape(local, orders_p + 8, wide)],
        [pltpu.VMEM((cells_x, 7, depth, lanes), F32)],
    )
    got_c = swap(to_c, "gy", 0)
    got_d = swap(to_d, "gy", 1)
    got_a = swap(to_a, "gx", 0)
    got_b = swap(to_b, "gx", 1)
    edges = jnp.stack((got_c, got_d))
    edge_a = swap(edges, "gx", 0)
    edge_b = swap(edges, "gx", 1)
    packs = [my_pack]
    for by in range(1, tiles_y):
        packs.append(cyclic(my_pack, "gy", by))

    span = cells_x + 2 * halo
    state = pltpu.VMEM((6, span, depth, 2 * lanes), F32)
    gate = pltpu.VMEM((span, 1, 2 * lanes), F32)
    coef_shape = shape(span, depth, 2 * lanes)
    phase_shape = shape(4 * cells_x, lanes)
    send_shape = shape(halo + 1, 6, depth, lanes)
    own, keep, curl, phase, to_a, to_b = call(
        functools.partial(first_kernel, geo=geo, total_x=total_x, total_y=total_y, count=count),
        [(flat_fields, "h"), (flat_map, "h"), (got_a, "v"), (got_b, "v"), (got_c, "v"), (got_d, "v"),
         (edge_a, "v"), (edge_b, "v"), (tables, "s"), (moments, "s")],
        [shape(6, cells_x, depth, 2 * lanes), coef_shape, coef_shape, phase_shape, send_shape, send_shape],
        [state, gate],
    )
    got_a = swap(to_a, "gx", 0)
    got_b = swap(to_b, "gx", 1)
    final, phase = call(
        functools.partial(second_kernel, geo=geo, total_x=total_x, total_y=total_y, count=count),
        [(own, "v"), (keep, "v"), (curl, "v"), (phase, "v"), (got_a, "v"), (got_b, "v"), (moments, "s")],
        [shape(6, depth * cells_x, lanes), phase_shape],
        [state, gate],
    )
    reach = orders_p + 2 * REACH
    ids_p = np.arange(-REACH, orders_p + REACH) % orders_p - orders_p // 2
    ids_q = np.arange(-REACH, orders_q + REACH) % orders_q - orders_q // 2
    cos_y, sin_y = waves(ids_q, np.arange(total_y), total_y)
    table_y = np.zeros((total_y, 2 * wide), np.float32)
    table_y[:, : len(ids_q)] = cos_y.T
    table_y[:, wide : wide + len(ids_q)] = sin_y.T
    cos_x, sin_x = waves(ids_p, np.arange(total_x), total_x)
    table_x = np.concatenate((cos_x, sin_x), 0).astype(np.float32)
    pixels = M
    cos_u, sin_u = waves(np.arange(orders_p) - orders_p // 2, np.arange(pixels), pixels)
    strip = pixels // (tiles_x * tiles_y)
    row_table = (np.concatenate((cos_u, sin_u), 0).T / math.sqrt(orders_p)).astype(np.float32)
    row_table = row_table.reshape(tiles_x * tiles_y, strip, 2 * orders_p).astype(jnp.bfloat16)
    cos_v, sin_v = waves(np.arange(orders_q) - orders_q // 2, np.arange(pixels), pixels)
    g_matrix = np.zeros((2 * wide, 2 * pixels), np.float32)
    g_matrix[:orders_q, :pixels] = cos_v / math.sqrt(orders_q)
    g_matrix[:orders_q, pixels:] = sin_v / math.sqrt(orders_q)
    g_matrix[wide : wide + orders_q, :pixels] = -sin_v / math.sqrt(orders_q)
    g_matrix[wide : wide + orders_q, pixels:] = cos_v / math.sqrt(orders_q)
    g_matrix = g_matrix.astype(jnp.bfloat16)

    pieces = [phase] + [cyclic(phase, "gy", by) for by in range(1, tiles_y)]
    part, final = call(
        functools.partial(along_y_kernel, count=tiles_y),
        [(piece, "v") for piece in pieces]
        + [(jnp.asarray(table_y.reshape(tiles_y, lanes, 2 * wide)), "h"), (final, "v")],
        [shape(2 * cells_x, 2 * wide), jax.ShapeDtypeStruct(final.shape, F32)],
        [pltpu.SemaphoreType.DMA],
    )
    parts = [part] + [cyclic(part, "gx", by) for by in range(1, tiles_x)]

    facts = jnp.concatenate([pack[:, orders_p, 0:3] for pack in packs], 0)
    shifts = facts[:, 0:2].astype(jnp.int32)
    weights = facts[:, 2]
    strips = call(
        functools.partial(
            image_kernel,
            tiles_x=tiles_x,
            tiles_y=tiles_y,
            cells_x=cells_x,
            scaling=1.0 / math.sqrt(total_x * total_y * STEPS),
            sources_all=local * tiles_x * tiles_y,
        ),
        [(piece, "v") for piece in parts]
        + [(pack, "v") for pack in packs]
        + [(jnp.asarray(table_x), "h"), (jnp.asarray(g_matrix), "h"), (jnp.asarray(row_table), "h"),
           (shifts, "s"), (weights, "s")],
        [shape(strip, pixels) for _ in range(tiles_x)],
        [
            pltpu.VMEM((2, total_x, 2 * wide), F32),
            pltpu.VMEM((4, reach, wide), F32),
            pltpu.VMEM((2 * orders_p, 4 * pixels), BF16),
            pltpu.VMEM((tiles_x * strip, 2 * orders_p), BF16),
            pltpu.VMEM((tiles_x * strip, pixels), F32),
        ],
    )
    image = strips[0]
    for by in range(1, tiles_x):
        image = image + cyclic(strips[by], "gx", by)
    return (final.reshape(fields.shape), image)


def solution(mesh):
    placed = (
        P("clips", None, "gx", "gy"),
        P("clips", "gx", "gy"),
        P(),
        P(),
        P(("gx", "gy"), None),
        P(("gx", "gy"), None, None),
        P(("gx", "gy")),
    )

    return jax.shard_map(
        body,
        mesh=mesh,
        in_specs=placed,
        out_specs=(P("clips", None, "gx", "gy"), P(("gx", "gy"), "clips")),
        check_vma=False,
    )
```

```python
import functools
import math

import jax
import jax.numpy as jnp
import numpy as np
from jax import lax
from jax.experimental import pallas as pl
from jax.experimental.pallas import tpu as pltpu
from jax.sharding import PartitionSpec as P

STEPS = 12
ROUNDS = 2
M = 512
REACH = 8

COURANT = 0.55
ANGULAR = 0.7
PRECISE = lax.Precision.HIGHEST


F32 = jnp.float32
BF16 = jnp.bfloat16


def vmem():
    return pl.BlockSpec(memory_space=pltpu.VMEM)


def smem():
    return pl.BlockSpec(memory_space=pltpu.SMEM)


def hbm():
    return pl.BlockSpec(memory_space=pltpu.HBM)


def call(kernel, ins, outs, scratch=(), limit=16):
    spaces = {"h": hbm, "c": vmem, "v": vmem, "s": smem}
    memories = {"h": pltpu.HBM, "v": pltpu.VMEM}

    def out_spec(out):
        return vmem() if not isinstance(out, jax.ShapeDtypeStruct) else pl.BlockSpec(memory_space=pl.ANY)

    held = [
        pltpu.with_memory_space_constraint(array, memories[space]) if space in memories else array
        for array, space in ins
    ]
    return pl.pallas_call(
        kernel,
        out_shape=outs,
        in_specs=[spaces[space]() for _, space in ins],
        out_specs=[out_spec(out) for out in outs],
        scratch_shapes=list(scratch),
        compiler_params=pltpu.CompilerParams(vmem_limit_bytes=limit << 20),
    )(*held)


def shape(*dims, dtype=F32):
    return pltpu.VMEM(dims, dtype)


def swap(values, axis, first):
    count = lax.axis_size(axis)
    pairs = []
    for low in range(first, count - 1, 2):
        pairs += [(low, low + 1), (low + 1, low)]
    if not pairs:
        return jnp.zeros_like(values)
    return lax.ppermute(values, axis, pairs)


def cyclic(values, axis, by):
    count = lax.axis_size(axis)
    return lax.ppermute(values, axis, [(i, (i + by) % count) for i in range(count)])


def waves(order_ids, cell_ids, period):
    wrapped = (order_ids[:, None] * cell_ids[None, :]) % period
    angles = 2.0 * math.pi / period * wrapped
    return np.cos(angles), np.sin(angles)


def pack_kernel(
    far_fields, far_map, shifts, weights, far_masks,
    fields, materials, send_a, send_b, send_c, send_d, source_pack,
    rows, masks, arrived, *, geo,
):
    copies = [
        pltpu.make_async_copy(far_fields, fields, arrived.at[0]),
        pltpu.make_async_copy(far_map, materials, arrived.at[1]),
        pltpu.make_async_copy(far_masks, masks, arrived.at[2]),
    ]
    for copy in copies:
        copy.start()
    for copy in copies:
        copy.wait()
    depth, cells_x, lanes, halo, slot = geo
    even_x = lax.axis_index("gx") % 2 == 0
    even_y = lax.axis_index("gy") % 2 == 0
    lane = lax.broadcasted_iota(jnp.int32, (depth, lanes), 1)
    for comp in range(7):
        high = jnp.zeros((depth, lanes), F32)
        low = jnp.zeros((depth, lanes), F32)
        for x in range(cells_x):
            if comp < 6:
                values = fields[comp, pl.ds(x, depth, stride=cells_x), :]
            else:
                values = materials[pl.ds(x, depth, stride=cells_x), :].astype(F32)
            rows[x, comp] = values
            here = (lane >= slot * x) & (lane < slot * (x + 1))
            high = jnp.where(here, pltpu.roll(values, (slot * x + slot) % lanes, 1), high)
            low = jnp.where(here, pltpu.roll(values, slot * x, 1) if x else values, low)
        send_c[comp] = jnp.where(even_y, high, low)
        send_d[comp] = jnp.where(even_y, low, high)
    far = cells_x - halo
    send_a[...] = rows[pl.ds(jnp.where(even_x, far, 0), halo)]
    send_b[...] = rows[pl.ds(jnp.where(even_x, 0, far), halo)]
    orders_p, orders_q = masks.shape[1:]
    source_pack[...] = jnp.zeros(source_pack.shape, F32)
    for source in range(masks.shape[0]):
        source_pack[source, 0:orders_p, 0:orders_q] = masks[source].astype(F32)
        for at, fact in enumerate((shifts[0, source], shifts[1, source], weights[source])):
            source_pack[source, orders_p : orders_p + 1, at : at + 1] = jnp.full((1, 1), fact).astype(F32)


def inside_lanes(lane, cells_y, total_y, slot):
    start = lax.axis_index("gy") * cells_y
    ring = 2 * cells_y
    place = start + jnp.where(lane < cells_y + slot, lane, lane - ring)
    held = (lane < cells_y + slot) | (lane >= ring - slot)
    return held & (place >= 0) & (place < total_y)


def run_steps(state, keep, curl, gate, phase, moments, first_step, geo, count):
    depth, cells_x, lanes, halo, _ = geo
    ring = 2 * lanes
    middle = depth // 2
    level = lax.broadcasted_iota(jnp.int32, (depth, ring), 0)
    at_top = level == depth - 1
    at_bottom = level == 0

    def next_y(values):
        return pltpu.roll(values, ring - 1, 1)

    def last_y(values):
        return pltpu.roll(values, 1, 1)

    def next_z(values):
        return jnp.where(at_top, 0.0, pltpu.roll(values, depth - 1, 0))

    def last_z(values):
        return jnp.where(at_bottom, 0.0, pltpu.roll(values, 1, 0))

    def step(index, carry):
        def row(i, inner):
            ex, ey, ez = state[0, i], state[1, i], state[2, i]
            open_h = gate[i]
            hx = state[3, i] - open_h * ((next_y(ez) - ez) - (next_z(ey) - ey))
            hy = state[4, i] - open_h * ((next_z(ex) - ex) - (state[2, i + 1] - ez))
            hz = state[5, i] - open_h * ((state[1, i + 1] - ey) - (next_y(ex) - ex))
            state[3, i] = hx
            state[4, i] = hy
            state[5, i] = hz
            before = jnp.maximum(i - 1, 0)
            kept, turned = keep[i], curl[i]
            state[0, i] = kept * ex + turned * ((hz - last_y(hz)) - (hy - last_z(hy)))
            state[1, i] = kept * ey + turned * ((hx - last_z(hx)) - (hz - state[5, before]))
            state[2, i] = kept * ez + turned * ((hy - state[4, before]) - (hx - last_y(hx)))
            return inner

        lax.fori_loop(index, cells_x + 2 * halo - 1 - index, row, 0)
        at = first_step + index
        cosine, sine = moments[at, 0], moments[at, 1]
        for comp in range(2):
            monitor = state[comp, halo : halo + cells_x, middle, 0:lanes]
            low = comp * cells_x
            phase[low : low + cells_x, :] = phase[low : low + cells_x, :] + monitor * cosine
            low = (2 + comp) * cells_x
            phase[low : low + cells_x, :] = phase[low : low + cells_x, :] - monitor * sine
        return carry

    lax.fori_loop(0, count, step, 0)


def set_gate(gate, geo, total_x, total_y):
    _, cells_x, lanes, halo, slot = geo
    lane = lax.broadcasted_iota(jnp.int32, (1, 2 * lanes), 1)
    held = jnp.where(inside_lanes(lane, lanes, total_y, slot), COURANT, 0.0).astype(F32)
    start = lax.axis_index("gx") * cells_x - halo
    for i in range(cells_x + 2 * halo):
        place = start + i
        gate[i] = jnp.where((place >= 0) & (place < total_x), held, 0.0)


def first_kernel(
    fields, materials, got_a, got_b, got_c, got_d, edge_a, edge_b, tables, moments,
    own, keep, curl, phase, send_a, send_b,
    state, gate, *, geo, total_x, total_y, count,
):
    depth, cells_x, lanes, halo, slot = geo
    odd_x = lax.axis_index("gx") % 2 == 1
    even_y = lax.axis_index("gy") % 2 == 0
    lane = lax.broadcasted_iota(jnp.int32, (depth, lanes), 1)
    all_lane = lax.broadcasted_iota(jnp.int32, (1, 2 * lanes), 1)
    inside_y = inside_lanes(all_lane, lanes, total_y, slot)
    start_x = lax.axis_index("gx") * cells_x - halo
    set_gate(gate, geo, total_x, total_y)

    def side(left, right, row):
        right = pltpu.roll(right, (-slot * row) % lanes, 1)
        left = pltpu.roll(left, (lanes - slot - slot * row) % lanes, 1)
        return jnp.where(lane < slot, right, jnp.where(lane >= lanes - slot, left, 0.0))

    def place(comp, i, main, more):
        if comp < 6:
            state[comp, i, :, 0:lanes] = main
            state[comp, i, :, lanes : 2 * lanes] = more
            return
        kind = jnp.concatenate((main, more), 1)
        row_in = (start_x + i >= 0) & (start_x + i < total_x)
        kept = jnp.zeros(kind.shape, F32)
        turned = jnp.zeros(kind.shape, F32)
        here = inside_y & row_in
        for material in range(tables.shape[1]):
            match = (kind == float(material)) & here
            kept = jnp.where(match, tables[0, material], kept)
            turned = jnp.where(match, tables[1, material], turned)
        keep[i] = kept
        curl[i] = turned

    base_a = jnp.where(odd_x, 0, cells_x + halo)
    base_b = jnp.where(odd_x, cells_x + halo, 0)
    from_a = jnp.where(odd_x, cells_x - halo, 0)
    from_b = jnp.where(odd_x, 0, cells_x - halo)
    for comp in range(7):
        c_pack, d_pack = got_c[comp], got_d[comp]
        left = jnp.where(even_y, d_pack, c_pack)
        right = jnp.where(even_y, c_pack, d_pack)
        for x in range(cells_x):
            if comp < 6:
                main = fields[comp, pl.ds(x, depth, stride=cells_x), :]
            else:
                main = materials[pl.ds(x, depth, stride=cells_x), :].astype(F32)
            place(comp, halo + x, main, side(left, right, x))
        for got, edge, base, origin in (
            (got_a, edge_a, base_a, from_a),
            (got_b, edge_b, base_b, from_b),
        ):
            c_pack, d_pack = edge[0, comp], edge[1, comp]
            left = jnp.where(even_y, d_pack, c_pack)
            right = jnp.where(even_y, c_pack, d_pack)
            for r in range(halo):
                place(comp, base + r, got[r, comp], side(left, right, origin + r))

    phase[...] = jnp.zeros(phase.shape, F32)
    run_steps(state, keep, curl, gate, phase, moments, 0, geo, count)

    for comp in range(6):
        own[comp] = state[comp, halo : halo + cells_x]
    width = lanes // cells_x
    for send, first in ((send_a, base_b), (send_b, base_a)):
        origin = jnp.where(first == 0, cells_x, halo)
        for comp in range(6):
            edges = jnp.zeros((depth, lanes), F32)
            for r in range(halo):
                send[r, comp] = state[comp, origin + r, :, 0:lanes]
                more = state[comp, origin + r, :, lanes : 2 * lanes]
                here = (lane >= width * r) & (lane < width * (r + 1))
                edges = jnp.where(here, pltpu.roll(more, (width * r + width // 2) % lanes, 1), edges)
            send[halo, comp] = edges


def second_kernel(
    own, keep, curl, phase_in, got_a, got_b, moments,
    final, phase,
    state, gate, *, geo, total_x, total_y, count,
):
    depth, cells_x, lanes, halo, _ = geo
    odd_x = lax.axis_index("gx") % 2 == 1
    lane = lax.broadcasted_iota(jnp.int32, (depth, lanes), 1)
    set_gate(gate, geo, total_x, total_y)
    base_a = jnp.where(odd_x, 0, cells_x + halo)
    base_b = jnp.where(odd_x, cells_x + halo, 0)
    width = lanes // cells_x
    half = width // 2
    edge = (lane < half) | (lane >= lanes - half)
    for comp in range(6):
        state[comp, halo : halo + cells_x] = own[comp]
        for got, base in ((got_a, base_a), (got_b, base_b)):
            pack = got[halo, comp]
            for r in range(halo):
                state[comp, base + r, :, 0:lanes] = got[r, comp]
                more = pltpu.roll(pack, (-(width * r + half)) % lanes, 1)
                state[comp, base + r, :, lanes : 2 * lanes] = jnp.where(edge, more, 0.0)
    phase[...] = phase_in[...]
    run_steps(state, keep, curl, gate, phase, moments, count, geo, count)
    for comp in range(6):
        for x in range(cells_x):
            final[comp, pl.ds(x, depth, stride=cells_x), :] = state[comp, halo + x, :, 0:lanes]


def along_y_kernel(*refs, count):
    pieces, (table, fields, part, kept, done) = refs[:count], refs[count:]
    keeping = pltpu.make_async_copy(fields, kept, done)
    keeping.start()
    me = lax.axis_index("gy")
    total = None
    for back, piece in enumerate(pieces):
        origin = (me - back + count) % count
        term = jnp.dot(piece[...], table[origin], precision=PRECISE, preferred_element_type=F32)
        total = term if total is None else total + term
    rows, width = total.shape[0] // 2, total.shape[1] // 2
    re_cos, re_sin = total[:rows, :width], total[:rows, width:]
    im_cos, im_sin = total[rows:, :width], total[rows:, width:]
    part[:, 0:width] = re_cos + im_sin
    part[:, width : 2 * width] = im_cos - re_sin
    keeping.wait()


def image_kernel(*refs, tiles_x, tiles_y, cells_x, scaling, sources_all):
    parts, refs = refs[:tiles_x], refs[tiles_x:]
    packs, refs = refs[:tiles_y], refs[tiles_y:]
    table_x, g_matrix, row_table, shifts, weights = refs[:5]
    strips, refs = refs[5 : 5 + tiles_x], refs[5 + tiles_x :]
    gathered, orders, columns, rows, total = refs
    me_x = lax.axis_index("gx")
    me_y = lax.axis_index("gy")
    width = orders.shape[2]
    reach = orders.shape[1]
    for back, part in enumerate(parts):
        origin = pl.multiple_of((me_x - back + tiles_x) % tiles_x * cells_x, cells_x)
        for comp in range(2):
            gathered[comp, pl.ds(origin, cells_x), :] = part[comp * cells_x : (comp + 1) * cells_x, :]
    for comp in range(2):
        re, im = gathered[comp, :, 0:width], gathered[comp, :, width : 2 * width]
        dot = functools.partial(jnp.dot, precision=PRECISE, preferred_element_type=F32)
        cos_x, sin_x = table_x[0:reach, :], table_x[reach : 2 * reach, :]
        order_re = dot(cos_x, re) + dot(sin_x, im)
        order_im = dot(cos_x, im) - dot(sin_x, re)
        orders[2 * comp] = (order_re * scaling).astype(BF16).astype(F32)
        orders[2 * comp + 1] = (order_im * scaling).astype(BF16).astype(F32)
    strip = row_table.shape[1]
    for ahead in range(tiles_x):
        owner = (me_x + ahead) % tiles_x * tiles_y + me_y
        rows[strip * ahead : strip * (ahead + 1), :] = row_table[owner]
    pixels = g_matrix.shape[1] // 2
    orders_p = rows.shape[1] // 2
    local = packs[0].shape[0]
    total[...] = jnp.zeros(total.shape, F32)
    for at, pack in enumerate(packs):

        def source(index, carry, at=at, pack=pack):
            number = at * local + index
            down = shifts[number, 0] + REACH
            across = width - (shifts[number, 1] + REACH)
            passed = pack[index, 0:orders_p, :]
            masked = []
            for plane in range(4):
                window = orders[plane, pl.ds(down, orders_p), :]
                masked.append((pltpu.roll(window, across, 1) * passed).astype(BF16))
            halves = jnp.concatenate(
                (jnp.concatenate(masked[:2], 1), jnp.concatenate(masked[2:], 1)), 0
            )
            spread = jnp.dot(halves, g_matrix[...], preferred_element_type=F32).astype(BF16)
            for comp in range(2):
                part = spread[comp * orders_p : (comp + 1) * orders_p]
                real, imag = part[:, :pixels], part[:, pixels:]
                low = 2 * comp * pixels
                columns[0:orders_p, low : low + pixels] = real
                columns[0:orders_p, low + pixels : low + 2 * pixels] = imag
                columns[orders_p : 2 * orders_p, low : low + pixels] = -imag
                columns[orders_p : 2 * orders_p, low + pixels : low + 2 * pixels] = real
            bright = None
            for block in range(4):
                value = jnp.dot(
                    rows[...],
                    columns[:, block * pixels : (block + 1) * pixels],
                    preferred_element_type=F32,
                )
                bright = value * value if bright is None else bright + value * value
            total[...] = total[...] + (weights[number] / sources_all) * bright
            return carry

        lax.fori_loop(0, local, source, 0)
    for ahead in range(tiles_x):
        strips[ahead][...] = total[strip * ahead : strip * (ahead + 1), :]


def body(
    fields, material_map, material_eps, material_loss, source_shift, source_mask, source_weight
):
    tiles_x = lax.axis_size("gx")
    tiles_y = lax.axis_size("gy")
    _, depth, cells_x, lanes = fields.shape
    total_x, total_y = cells_x * tiles_x, lanes * tiles_y
    count = STEPS // ROUNDS
    halo = count
    slot = lanes // cells_x
    assert halo <= cells_x and slot >= STEPS and slot // 2 >= halo
    geo = (depth, cells_x, lanes, halo, slot)
    flat_fields = fields.reshape(6, depth * cells_x, lanes)
    flat_map = material_map.reshape(depth * cells_x, lanes)
    local, orders_p, orders_q = source_mask.shape
    wide = 128

    keep_table = (1.0 - material_loss) / (1.0 + material_loss)
    curl_table = COURANT / (material_eps * (1.0 + material_loss))
    tables = jnp.stack((keep_table, curl_table))
    angle = np.float32(ANGULAR) * np.arange(1, STEPS + 1, dtype=np.float32)
    moments = jnp.asarray(np.stack((np.cos(angle), np.sin(angle)), 1).astype(np.float32))

    row_shape = shape(halo, 7, depth, lanes)
    edge_shape = shape(7, depth, lanes)
    near_fields, near_map, to_a, to_b, to_c, to_d, my_pack = call(
        functools.partial(pack_kernel, geo=geo),
        [(flat_fields, "h"), (flat_map, "h"), (source_shift.T, "s"), (source_weight, "s"), (source_mask, "h")],
        [shape(*flat_fields.shape), shape(*flat_map.shape, dtype=jnp.int32)]
        + [row_shape, row_shape, edge_shape, edge_shape, shape(local, orders_p + 8, wide)],
        [
            pltpu.VMEM((cells_x, 7, depth, lanes), F32),
            pltpu.VMEM(source_mask.shape, jnp.int32),
            pltpu.SemaphoreType.DMA((3,)),
        ],
    )
    got_c = swap(to_c, "gy", 0)
    got_d = swap(to_d, "gy", 1)
    got_a = swap(to_a, "gx", 0)
    got_b = swap(to_b, "gx", 1)
    edges = jnp.stack((got_c, got_d))
    edge_a = swap(edges, "gx", 0)
    edge_b = swap(edges, "gx", 1)
    packs = [my_pack]
    for by in range(1, tiles_y):
        packs.append(cyclic(my_pack, "gy", by))

    span = cells_x + 2 * halo
    state = pltpu.VMEM((6, span, depth, 2 * lanes), F32)
    gate = pltpu.VMEM((span, 1, 2 * lanes), F32)
    coef_shape = shape(span, depth, 2 * lanes)
    phase_shape = shape(4 * cells_x, lanes)
    send_shape = shape(halo + 1, 6, depth, lanes)
    own, keep, curl, phase, to_a, to_b = call(
        functools.partial(first_kernel, geo=geo, total_x=total_x, total_y=total_y, count=count),
        [(near_fields, "v"), (near_map, "v"), (got_a, "v"), (got_b, "v"), (got_c, "v"), (got_d, "v"),
         (edge_a, "v"), (edge_b, "v"), (tables, "s"), (moments, "s")],
        [shape(6, cells_x, depth, 2 * lanes), coef_shape, coef_shape, phase_shape, send_shape, send_shape],
        [state, gate],
    )
    got_a = swap(to_a, "gx", 0)
    got_b = swap(to_b, "gx", 1)
    final, phase = call(
        functools.partial(second_kernel, geo=geo, total_x=total_x, total_y=total_y, count=count),
        [(own, "v"), (keep, "v"), (curl, "v"), (phase, "v"), (got_a, "v"), (got_b, "v"), (moments, "s")],
        [shape(6, depth * cells_x, lanes), phase_shape],
        [state, gate],
    )
    reach = orders_p + 2 * REACH
    ids_p = np.arange(-REACH, orders_p + REACH) % orders_p - orders_p // 2
    ids_q = np.arange(-REACH, orders_q + REACH) % orders_q - orders_q // 2
    cos_y, sin_y = waves(ids_q, np.arange(total_y), total_y)
    table_y = np.zeros((total_y, 2 * wide), np.float32)
    table_y[:, : len(ids_q)] = cos_y.T
    table_y[:, wide : wide + len(ids_q)] = sin_y.T
    cos_x, sin_x = waves(ids_p, np.arange(total_x), total_x)
    table_x = np.concatenate((cos_x, sin_x), 0).astype(np.float32)
    pixels = M
    cos_u, sin_u = waves(np.arange(orders_p) - orders_p // 2, np.arange(pixels), pixels)
    strip = pixels // (tiles_x * tiles_y)
    row_table = (np.concatenate((cos_u, sin_u), 0).T / math.sqrt(orders_p)).astype(np.float32)
    row_table = row_table.reshape(tiles_x * tiles_y, strip, 2 * orders_p).astype(jnp.bfloat16)
    cos_v, sin_v = waves(np.arange(orders_q) - orders_q // 2, np.arange(pixels), pixels)
    g_matrix = np.zeros((2 * wide, 2 * pixels), np.float32)
    g_matrix[:orders_q, :pixels] = cos_v / math.sqrt(orders_q)
    g_matrix[:orders_q, pixels:] = sin_v / math.sqrt(orders_q)
    g_matrix[wide : wide + orders_q, :pixels] = -sin_v / math.sqrt(orders_q)
    g_matrix[wide : wide + orders_q, pixels:] = cos_v / math.sqrt(orders_q)
    g_matrix = g_matrix.astype(jnp.bfloat16)

    pieces = [phase] + [cyclic(phase, "gy", by) for by in range(1, tiles_y)]
    part, final = call(
        functools.partial(along_y_kernel, count=tiles_y),
        [(piece, "v") for piece in pieces]
        + [(jnp.asarray(table_y.reshape(tiles_y, lanes, 2 * wide)), "c"), (final, "v")],
        [shape(2 * cells_x, 2 * wide), jax.ShapeDtypeStruct(final.shape, F32)],
        [pltpu.SemaphoreType.DMA],
    )
    parts = [part] + [cyclic(part, "gx", by) for by in range(1, tiles_x)]

    facts = jnp.concatenate([pack[:, orders_p, 0:3] for pack in packs], 0)
    shifts = facts[:, 0:2].astype(jnp.int32)
    weights = facts[:, 2]
    strips = call(
        functools.partial(
            image_kernel,
            tiles_x=tiles_x,
            tiles_y=tiles_y,
            cells_x=cells_x,
            scaling=1.0 / math.sqrt(total_x * total_y * STEPS),
            sources_all=local * tiles_x * tiles_y,
        ),
        [(piece, "v") for piece in parts]
        + [(pack, "v") for pack in packs]
        + [(jnp.asarray(table_x), "c"), (jnp.asarray(g_matrix), "c"), (jnp.asarray(row_table), "c"),
           (shifts, "s"), (weights, "s")],
        [shape(strip, pixels) for _ in range(tiles_x)],
        [
            pltpu.VMEM((2, total_x, 2 * wide), F32),
            pltpu.VMEM((4, reach, wide), F32),
            pltpu.VMEM((2 * orders_p, 4 * pixels), BF16),
            pltpu.VMEM((tiles_x * strip, 2 * orders_p), BF16),
            pltpu.VMEM((tiles_x * strip, pixels), F32),
        ],
    )
    image = strips[0]
    for by in range(1, tiles_x):
        image = image + cyclic(strips[by], "gx", by)
    return (final.reshape(fields.shape), image)


def solution(mesh):
    placed = (
        P("clips", None, "gx", "gy"),
        P("clips", "gx", "gy"),
        P(),
        P(),
        P(("gx", "gy"), None),
        P(("gx", "gy"), None, None),
        P(("gx", "gy")),
    )

    return jax.shard_map(
        body,
        mesh=mesh,
        in_specs=placed,
        out_specs=(P("clips", None, "gx", "gy"), P(("gx", "gy"), "clips")),
        check_vma=False,
    )
```

```python
import functools
import math

import jax
import jax.numpy as jnp
import numpy as np
from jax import lax
from jax.experimental import pallas as pl
from jax.experimental.pallas import tpu as pltpu
from jax.sharding import PartitionSpec as P

STEPS = 12
ROUNDS = 2
M = 512
REACH = 8

COURANT = 0.55
ANGULAR = 0.7
PRECISE = lax.Precision.HIGHEST


F32 = jnp.float32
BF16 = jnp.bfloat16


def vmem():
    return pl.BlockSpec(memory_space=pltpu.VMEM)


def smem():
    return pl.BlockSpec(memory_space=pltpu.SMEM)


def hbm():
    return pl.BlockSpec(memory_space=pltpu.HBM)


def call(kernel, ins, outs, scratch=(), limit=16):
    spaces = {"h": hbm, "c": vmem, "v": vmem, "s": smem}
    memories = {"h": pltpu.HBM, "v": pltpu.VMEM}

    def out_spec(out):
        return vmem() if not isinstance(out, jax.ShapeDtypeStruct) else pl.BlockSpec(memory_space=pl.ANY)

    held = [
        pltpu.with_memory_space_constraint(array, memories[space]) if space in memories else array
        for array, space in ins
    ]
    return pl.pallas_call(
        kernel,
        out_shape=outs,
        in_specs=[spaces[space]() for _, space in ins],
        out_specs=[out_spec(out) for out in outs],
        scratch_shapes=list(scratch),
        compiler_params=pltpu.CompilerParams(vmem_limit_bytes=limit << 20),
    )(*held)


def shape(*dims, dtype=F32):
    return pltpu.VMEM(dims, dtype)


def swap(values, axis, first):
    count = lax.axis_size(axis)
    pairs = []
    for low in range(first, count - 1, 2):
        pairs += [(low, low + 1), (low + 1, low)]
    if not pairs:
        return jnp.zeros_like(values)
    return lax.ppermute(values, axis, pairs)


def cyclic(values, axis, by):
    count = lax.axis_size(axis)
    return lax.ppermute(values, axis, [(i, (i + by) % count) for i in range(count)])


def waves(order_ids, cell_ids, period):
    wrapped = (order_ids[:, None] * cell_ids[None, :]) % period
    angles = 2.0 * math.pi / period * wrapped
    return np.cos(angles), np.sin(angles)


class Geo:
    def __init__(self, depth, cells_x, cells_y, total_x, total_y, count):
        self.depth, self.cells_x, self.cells_y = depth, cells_x, cells_y
        self.total_x, self.total_y, self.count = total_x, total_y, count
        self.wide = 128
        self.per = self.wide // depth
        self.own = cells_x // self.per
        self.groups = 3 * self.own
        self.pad = 16
        self.slack = 8
        self.first = self.slack + self.pad
        self.rows = cells_y + 2 * self.first
        self.half = self.wide // 2
        self.reach = 8
        assert self.per * depth == self.wide and self.own == 2 and cells_x == 2 * self.per
        assert self.per + self.per // 2 == count and STEPS <= self.pad and STEPS - count <= self.reach


PLANES = 6
SCALE = 1.0 / COURANT


def halves_of(planes):
    return (planes + 1) // 2


def pack_rows(get, put, planes, upper, lane, half):
    for plane in range(planes):
        put(plane, get(plane, 1 if upper else 0))
    kept = (lane >= half) if upper else (lane < half)
    group = 0 if upper else 1
    for at in range(halves_of(planes)):
        value = get(2 * at, group)
        if 2 * at + 1 < planes:
            value = jnp.where(kept, value, pltpu.roll(get(2 * at + 1, group), half, 1))
        put(planes + at, value)


def unpack_rows(get, put, planes, inner, outer, kept, half):
    for plane in range(planes):
        put(plane, inner, get(plane))
        value = get(planes + plane // 2)
        if plane % 2:
            value = pltpu.roll(value, half, 1)
        put(plane, outer, jnp.where(kept, value, 0.0))


def pack_kernel(
    far_fields, far_map, shifts, weights, far_masks,
    tile, send_a, send_b, send_c, send_d, source_pack,
    fields, materials, masks, arrived, *, geo,
):
    copies = [
        pltpu.make_async_copy(far_fields, fields, arrived.at[0]),
        pltpu.make_async_copy(far_map, materials, arrived.at[1]),
        pltpu.make_async_copy(far_masks, masks, arrived.at[2]),
    ]
    for copy in copies:
        copy.start()
    for copy in copies:
        copy.wait()
    even_x = lax.axis_index("gx") % 2 == 0
    even_y = lax.axis_index("gy") % 2 == 0
    pad, last = geo.pad, geo.cells_y - geo.pad
    for plane in range(PLANES + 1):
        for group in range(geo.own):
            parts = []
            for x in range(group * geo.per, (group + 1) * geo.per):
                here = pl.ds(x, geo.depth, stride=geo.cells_x)
                parts.append(fields[plane, here, :] if plane < PLANES else materials[here, :].astype(F32))
            values = jnp.concatenate(parts, 0).T
            if 3 <= plane < PLANES:
                values = values * SCALE
            tile[plane, group] = values
            low, high = values[0:pad], values[last:]
            send_c[plane, group] = jnp.where(even_y, high, low)
            send_d[plane, group] = jnp.where(even_y, low, high)
    lane = lax.broadcasted_iota(jnp.int32, (geo.cells_y, geo.wide), 1)

    def fill(send, upper):
        def put(at, value):
            send[at] = value

        pack_rows(lambda plane, group: tile[plane, group], put, PLANES + 1, upper, lane, geo.half)

    @pl.when(even_x)
    def _():
        fill(send_a, True)
        fill(send_b, False)

    @pl.when(jnp.logical_not(even_x))
    def _():
        fill(send_a, False)
        fill(send_b, True)

    orders_p, orders_q = masks.shape[1:]
    source_pack[...] = jnp.zeros(source_pack.shape, F32)
    for source in range(masks.shape[0]):
        source_pack[source, 0:orders_p, 0:orders_q] = masks[source].astype(F32)
        for at, fact in enumerate((shifts[0, source], shifts[1, source], weights[source])):
            source_pack[source, orders_p : orders_p + 1, at : at + 1] = jnp.full((1, 1), fact).astype(F32)


def edge_kernel(got_c, got_d, send_a, send_b, *, geo):
    even_x = lax.axis_index("gx") % 2 == 0
    even_y = lax.axis_index("gy") % 2 == 0
    lane = lax.broadcasted_iota(jnp.int32, (geo.pad, geo.wide), 1)

    def fill(send, upper):
        for side in range(2):

            def get(plane, group, side=side):
                c_value, d_value = got_c[plane, group], got_d[plane, group]
                if side:
                    return jnp.where(even_y, c_value, d_value)
                return jnp.where(even_y, d_value, c_value)

            def put(at, value, side=side):
                send[at, side * geo.pad : (side + 1) * geo.pad, :] = value

            pack_rows(get, put, PLANES + 1, upper, lane, geo.half)

    @pl.when(even_x)
    def _():
        fill(send_a, True)
        fill(send_b, False)

    @pl.when(jnp.logical_not(even_x))
    def _():
        fill(send_a, False)
        fill(send_b, True)


def run_steps(state, keep, curl, phase, moments, first_step, geo):
    ex, ey, ez, hx, hy, hz = state
    wide, depth, groups = geo.wide, geo.depth, geo.groups
    first = geo.first
    chunk = 16
    beyond = geo.pad if first_step == 0 else geo.reach
    starts = range(first - beyond, first + geo.cells_y + beyond, chunk)
    lane = lax.broadcasted_iota(jnp.int32, (chunk, wide), 1)
    level = lane % depth
    at_top, at_bottom = level == depth - 1, level == 0
    not_first, not_last = lane >= depth, lane < wide - depth
    low_x = lax.axis_index("gx") == 0
    low_y = lax.axis_index("gy") == 0

    def next_z(values):
        return jnp.where(at_top, 0.0, pltpu.roll(values, wide - 1, 1))

    def last_z(values):
        return jnp.where(at_bottom, 0.0, pltpu.roll(values, 1, 1))

    def magnetic(g, carry):
        after = jnp.minimum(g + 1, groups - 1)
        for start in starts:
            here, ahead = pl.ds(start, chunk), pl.ds(start + 1, chunk)
            x, y, z = ex[g, here, :], ey[g, here, :], ez[g, here, :]
            y_x = pltpu.roll(jnp.where(not_first, y, ey[after, here, :]), wide - depth, 1)
            z_x = pltpu.roll(jnp.where(not_first, z, ez[after, here, :]), wide - depth, 1)
            hx[g, here, :] = hx[g, here, :] - ((ez[g, ahead, :] - z) - (next_z(y) - y))
            hy[g, here, :] = hy[g, here, :] - ((next_z(x) - x) - (z_x - z))
            hz[g, here, :] = hz[g, here, :] - ((y_x - y) - (ex[g, ahead, :] - x))
        return carry

    def electric(g, carry):
        before = jnp.maximum(g - 1, 0)
        for start in starts:
            here, behind = pl.ds(start, chunk), pl.ds(start - 1, chunk)
            x, y, z = hx[g, here, :], hy[g, here, :], hz[g, here, :]
            y_x = pltpu.roll(jnp.where(not_last, y, hy[before, here, :]), depth, 1)
            z_x = pltpu.roll(jnp.where(not_last, z, hz[before, here, :]), depth, 1)
            row = pl.ds(start - first + geo.pad, chunk)
            kept, turned = keep[g, row, :], curl[g, row, :]
            ex[g, here, :] = kept * ex[g, here, :] + turned * ((z - hz[g, behind, :]) - (y - last_z(y)))
            ey[g, here, :] = kept * ey[g, here, :] + turned * ((x - last_z(x)) - (z - z_x))
            ez[g, here, :] = kept * ez[g, here, :] + turned * ((y - y_x) - (x - hx[g, behind, :]))
        return carry

    near = geo.own * geo.per

    def step(index, carry):
        left = geo.count - 1 - index
        low = (near - left - 1) // geo.per
        high = (near + geo.cells_x - 1 + left) // geo.per + 1
        lax.fori_loop(low, high, magnetic, 0)

        @pl.when(low_y)
        def _():
            for field in (hx, hz):
                for g in range(groups):
                    field[g, first - 1 : first, :] = jnp.zeros((1, wide), F32)

        @pl.when(low_x)
        def _():
            for field in (hy, hz):
                for start in starts:
                    here = pl.ds(start, chunk)
                    field[geo.own - 1, here, :] = jnp.where(not_last, field[geo.own - 1, here, :], 0.0)

        lax.fori_loop(low, high, electric, 0)
        at = first_step + index
        cosine, sine = moments[at, 0], moments[at, 1]
        middle = depth // 2
        for start in range(0, geo.cells_y, chunk):
            here = pl.ds(first + start, chunk)
            seen = ex[geo.own, here, :]
            for spot, (field, g) in enumerate(((ex, 1), (ey, 0), (ey, 1)), 1):
                moved = pltpu.roll(field[geo.own + g, here, :], spot, 1)
                seen = jnp.where(level == middle + spot, moved, seen)
            there = pl.ds(start, chunk)
            phase[0, there, :] = phase[0, there, :] + seen * cosine
            phase[1, there, :] = phase[1, there, :] - seen * sine
        return carry

    lax.fori_loop(0, geo.count, step, 0)


def sides(geo):
    odd_x = lax.axis_index("gx") % 2 == 1
    below = (geo.own - 1, geo.own - 2)
    above = (2 * geo.own, 2 * geo.own + 1)
    return [
        (jnp.where(odd_x, below[0], above[0]), jnp.where(odd_x, below[1], above[1]), odd_x),
        (jnp.where(odd_x, above[0], below[0]), jnp.where(odd_x, above[1], below[1]), jnp.logical_not(odd_x)),
    ]


def clear(state, geo, beyond):
    low, high = geo.first - beyond, geo.first + geo.cells_y + beyond
    for field in state:
        for g in range(geo.groups):
            field[g, 0:low, :] = jnp.zeros((low, geo.wide), F32)
            field[g, high : geo.rows, :] = jnp.zeros((geo.rows - high, geo.wide), F32)


def half_lanes(rows, geo, lower):
    lane = lax.broadcasted_iota(jnp.int32, (rows, geo.wide), 1)
    return (lane >= geo.half) == lower


def first_kernel(
    tile, got_a, got_b, got_c, got_d, edge_a, edge_b, tables, moments,
    own, keep, curl, phase, send_a, send_b,
    ex, ey, ez, hx, hy, hz, kinds, *, geo,
):
    state = (ex, ey, ez, hx, hy, hz)
    planes = (*state, kinds)
    even_y = lax.axis_index("gy") % 2 == 0
    pad, first, cells_y = geo.pad, geo.first, geo.cells_y
    main = pl.ds(first, cells_y)
    spans = (pl.ds(first - pad, pad), pl.ds(first + cells_y, pad))
    clear(state, geo, pad)
    for at, plane in enumerate(planes):
        for group in range(geo.own):
            g = geo.own + group
            plane[g, main, :] = tile[at, group]
            c_value, d_value = got_c[at, group], got_d[at, group]
            plane[g, spans[0], :] = jnp.where(even_y, d_value, c_value)
            plane[g, spans[1], :] = jnp.where(even_y, c_value, d_value)
    for got, edge, (inner, outer, lower) in zip((got_a, got_b), (edge_a, edge_b), sides(geo)):

        def put_main(at, g, value):
            planes[at][g, main, :] = value

        unpack_rows(
            lambda at, got=got: got[at], put_main, PLANES + 1, inner, outer, half_lanes(cells_y, geo, lower), geo.half
        )
        for side in range(2):

            def put_side(at, g, value, side=side):
                planes[at][g, spans[side], :] = value

            unpack_rows(
                lambda at, edge=edge, side=side: edge[at, side * pad : (side + 1) * pad, :],
                put_side, PLANES + 1, inner, outer, half_lanes(pad, geo, lower), geo.half,
            )

    chunk = 16
    lane = lax.broadcasted_iota(jnp.int32, (chunk, geo.wide), 1)
    row = lax.broadcasted_iota(jnp.int32, (chunk, geo.wide), 0)
    base_x = (lax.axis_index("gx") - 1) * geo.cells_x
    base_y = lax.axis_index("gy") * cells_y - pad

    def coefs(g, carry):
        place_x = base_x + g * geo.per + lane // geo.depth
        inside_x = (place_x >= 0) & (place_x < geo.total_x)
        for start in range(0, cells_y + 2 * pad, chunk):
            place_y = base_y + start + row
            inside = inside_x & (place_y >= 0) & (place_y < geo.total_y)
            kind = kinds[g, pl.ds(first - pad + start, chunk), :]
            kept = jnp.zeros(kind.shape, F32)
            turned = jnp.zeros(kind.shape, F32)
            for material in range(tables.shape[1]):
                match = kind == float(material)
                kept = jnp.where(match, tables[0, material], kept)
                turned = jnp.where(match, tables[1, material], turned)
            there = pl.ds(start, chunk)
            keep[g, there, :] = jnp.where(inside, kept, 0.0)
            curl[g, there, :] = jnp.where(inside, turned, 0.0)
        return carry

    lax.fori_loop(0, geo.groups, coefs, 0)
    phase[...] = jnp.zeros(phase.shape, F32)
    run_steps(state, keep, curl, phase, moments, 0, geo)

    more = pl.ds(first - geo.reach, cells_y + 2 * geo.reach)
    lane = lax.broadcasted_iota(jnp.int32, (cells_y + 2 * geo.reach, geo.wide), 1)
    for at, field in enumerate(state):
        for group in range(geo.own):
            own[at, group] = field[geo.own + group, more, :]

    def fill(send, upper):
        def put(at, value):
            send[at] = value

        pack_rows(lambda at, group: own[at, group], put, PLANES, upper, lane, geo.half)

    even_x = lax.axis_index("gx") % 2 == 0

    @pl.when(even_x)
    def _():
        fill(send_a, True)
        fill(send_b, False)

    @pl.when(jnp.logical_not(even_x))
    def _():
        fill(send_a, False)
        fill(send_b, True)


def second_kernel(
    own, keep, curl, phase_in, got_a, got_b, moments,
    final, phase,
    ex, ey, ez, hx, hy, hz, seen, *, geo,
):
    state = (ex, ey, ez, hx, hy, hz)
    first, cells_y = geo.first, geo.cells_y
    rows = cells_y + 2 * geo.reach
    more = pl.ds(first - geo.reach, rows)
    clear(state, geo, geo.reach)
    for at, field in enumerate(state):
        for group in range(geo.own):
            field[geo.own + group, more, :] = own[at, group]
    for got, (inner, outer, lower) in zip((got_a, got_b), sides(geo)):

        def put(at, g, value):
            state[at][g, more, :] = value

        unpack_rows(lambda at, got=got: got[at], put, PLANES, inner, outer, half_lanes(rows, geo, lower), geo.half)
    seen[...] = phase_in[...]
    run_steps(state, keep, curl, seen, moments, geo.count, geo)
    middle = geo.depth // 2
    for part in range(2):
        turned = seen[part].T
        for within in range(geo.per):
            for comp in range(2):
                for group in range(geo.own):
                    source = within * geo.depth + middle + comp * geo.own + group
                    target = (part * 2 + comp) * geo.cells_x + group * geo.per + within
                    phase[target : target + 1, :] = turned[source : source + 1, :]
    for at, field in enumerate(state):
        for group in range(geo.own):
            values = field[geo.own + group, pl.ds(first, cells_y), :].T
            if at >= 3:
                values = values * COURANT
            for within in range(geo.per):
                here = pl.ds(group * geo.per + within, geo.depth, stride=geo.cells_x)
                final[at, here, :] = values[within * geo.depth : (within + 1) * geo.depth]


def along_y_kernel(*refs, count):
    pieces, (table, fields, part, kept, done) = refs[:count], refs[count:]
    keeping = pltpu.make_async_copy(fields, kept, done)
    keeping.start()
    me = lax.axis_index("gy")
    total = None
    for back, piece in enumerate(pieces):
        origin = (me - back + count) % count
        term = jnp.dot(piece[...], table[origin], precision=PRECISE, preferred_element_type=F32)
        total = term if total is None else total + term
    rows, width = total.shape[0] // 2, total.shape[1] // 2
    re_cos, re_sin = total[:rows, :width], total[:rows, width:]
    im_cos, im_sin = total[rows:, :width], total[rows:, width:]
    part[:, 0:width] = re_cos + im_sin
    part[:, width : 2 * width] = im_cos - re_sin
    keeping.wait()


def image_kernel(*refs, tiles_x, tiles_y, cells_x, scaling, sources_all):
    parts, refs = refs[:tiles_x], refs[tiles_x:]
    packs, refs = refs[:tiles_y], refs[tiles_y:]
    table_x, g_matrix, row_table, shifts, weights = refs[:5]
    strips, refs = refs[5 : 5 + tiles_x], refs[5 + tiles_x :]
    gathered, orders, columns, rows, total = refs
    me_x = lax.axis_index("gx")
    me_y = lax.axis_index("gy")
    width = orders.shape[2]
    reach = orders.shape[1]
    for back, part in enumerate(parts):
        origin = pl.multiple_of((me_x - back + tiles_x) % tiles_x * cells_x, cells_x)
        for comp in range(2):
            gathered[comp, pl.ds(origin, cells_x), :] = part[comp * cells_x : (comp + 1) * cells_x, :]
    for comp in range(2):
        re, im = gathered[comp, :, 0:width], gathered[comp, :, width : 2 * width]
        dot = functools.partial(jnp.dot, precision=PRECISE, preferred_element_type=F32)
        cos_x, sin_x = table_x[0:reach, :], table_x[reach : 2 * reach, :]
        order_re = dot(cos_x, re) + dot(sin_x, im)
        order_im = dot(cos_x, im) - dot(sin_x, re)
        orders[2 * comp] = (order_re * scaling).astype(BF16).astype(F32)
        orders[2 * comp + 1] = (order_im * scaling).astype(BF16).astype(F32)
    strip = row_table.shape[1]
    for ahead in range(tiles_x):
        owner = (me_x + ahead) % tiles_x * tiles_y + me_y
        rows[strip * ahead : strip * (ahead + 1), :] = row_table[owner]
    pixels = g_matrix.shape[1] // 2
    orders_p = rows.shape[1] // 2
    local = packs[0].shape[0]
    total[...] = jnp.zeros(total.shape, F32)
    for at, pack in enumerate(packs):

        def source(index, carry, at=at, pack=pack):
            number = at * local + index
            down = shifts[number, 0] + REACH
            across = width - (shifts[number, 1] + REACH)
            passed = pack[index, 0:orders_p, :]
            masked = []
            for plane in range(4):
                window = orders[plane, pl.ds(down, orders_p), :]
                masked.append((pltpu.roll(window, across, 1) * passed).astype(BF16))
            halves = jnp.concatenate(
                (jnp.concatenate(masked[:2], 1), jnp.concatenate(masked[2:], 1)), 0
            )
            spread = jnp.dot(halves, g_matrix[...], preferred_element_type=F32).astype(BF16)
            for comp in range(2):
                part = spread[comp * orders_p : (comp + 1) * orders_p]
                real, imag = part[:, :pixels], part[:, pixels:]
                low = 2 * comp * pixels
                columns[0:orders_p, low : low + pixels] = real
                columns[0:orders_p, low + pixels : low + 2 * pixels] = imag
                columns[orders_p : 2 * orders_p, low : low + pixels] = -imag
                columns[orders_p : 2 * orders_p, low + pixels : low + 2 * pixels] = real
            bright = None
            for block in range(4):
                value = jnp.dot(
                    rows[...],
                    columns[:, block * pixels : (block + 1) * pixels],
                    preferred_element_type=F32,
                )
                bright = value * value if bright is None else bright + value * value
            total[...] = total[...] + (weights[number] / sources_all) * bright
            return carry

        lax.fori_loop(0, local, source, 0)
    for ahead in range(tiles_x):
        strips[ahead][...] = total[strip * ahead : strip * (ahead + 1), :]


def body(
    fields, material_map, material_eps, material_loss, source_shift, source_mask, source_weight
):
    tiles_x = lax.axis_size("gx")
    tiles_y = lax.axis_size("gy")
    _, depth, cells_x, lanes = fields.shape
    total_x, total_y = cells_x * tiles_x, lanes * tiles_y
    count = STEPS // ROUNDS
    geo = Geo(depth, cells_x, lanes, total_x, total_y, count)
    flat_fields = fields.reshape(6, depth * cells_x, lanes)
    flat_map = material_map.reshape(depth * cells_x, lanes)
    local, orders_p, orders_q = source_mask.shape
    wide = 128

    keep_table = (1.0 - material_loss) / (1.0 + material_loss)
    curl_table = COURANT * (COURANT / (material_eps * (1.0 + material_loss)))
    tables = jnp.stack((keep_table, curl_table))
    angle = np.float32(ANGULAR) * np.arange(1, STEPS + 1, dtype=np.float32)
    moments = jnp.asarray(np.stack((np.cos(angle), np.sin(angle)), 1).astype(np.float32))

    sent = PLANES + 1 + halves_of(PLANES + 1)
    row_shape = shape(sent, lanes, wide)
    side_shape = shape(PLANES + 1, geo.own, geo.pad, wide)
    edge_shape = shape(sent, 2 * geo.pad, wide)
    tile, to_a, to_b, to_c, to_d, my_pack = call(
        functools.partial(pack_kernel, geo=geo),
        [(flat_fields, "h"), (flat_map, "h"), (source_shift.T, "s"), (source_weight, "s"), (source_mask, "h")],
        [shape(PLANES + 1, geo.own, lanes, wide), row_shape, row_shape, side_shape, side_shape]
        + [shape(local, orders_p + 8, wide)],
        [
            pltpu.VMEM(flat_fields.shape, F32),
            pltpu.VMEM(flat_map.shape, jnp.int32),
            pltpu.VMEM(source_mask.shape, jnp.int32),
            pltpu.SemaphoreType.DMA((3,)),
        ],
    )
    got_c = swap(to_c, "gy", 0)
    got_d = swap(to_d, "gy", 1)
    got_a = swap(to_a, "gx", 0)
    got_b = swap(to_b, "gx", 1)
    to_a, to_b = call(functools.partial(edge_kernel, geo=geo), [(got_c, "v"), (got_d, "v")], [edge_shape, edge_shape])
    edge_a = swap(to_a, "gx", 0)
    edge_b = swap(to_b, "gx", 1)
    packs = [my_pack]
    for by in range(1, tiles_y):
        packs.append(cyclic(my_pack, "gy", by))

    state = [pltpu.VMEM((geo.groups, geo.rows, wide), F32) for _ in range(PLANES)]
    coef_shape = shape(geo.groups, lanes + 2 * geo.pad, wide)
    seen_shape = shape(2, lanes, wide)
    longer = lanes + 2 * geo.reach
    send_shape = shape(PLANES + halves_of(PLANES), longer, wide)
    own, keep, curl, seen, to_a, to_b = call(
        functools.partial(first_kernel, geo=geo),
        [(tile, "v"), (got_a, "v"), (got_b, "v"), (got_c, "v"), (got_d, "v"), (edge_a, "v"), (edge_b, "v"),
         (tables, "s"), (moments, "s")],
        [shape(PLANES, geo.own, longer, wide), coef_shape, coef_shape, seen_shape, send_shape, send_shape],
        [*state, pltpu.VMEM((geo.groups, geo.rows, wide), F32)],
    )
    got_a = swap(to_a, "gx", 0)
    got_b = swap(to_b, "gx", 1)
    final, phase = call(
        functools.partial(second_kernel, geo=geo),
        [(own, "v"), (keep, "v"), (curl, "v"), (seen, "v"), (got_a, "v"), (got_b, "v"), (moments, "s")],
        [shape(PLANES, depth * cells_x, lanes), shape(4 * cells_x, lanes)],
        [*state, pltpu.VMEM((2, lanes, wide), F32)],
    )

    reach = orders_p + 2 * REACH
    ids_p = np.arange(-REACH, orders_p + REACH) % orders_p - orders_p // 2
    ids_q = np.arange(-REACH, orders_q + REACH) % orders_q - orders_q // 2
    cos_y, sin_y = waves(ids_q, np.arange(total_y), total_y)
    table_y = np.zeros((total_y, 2 * wide), np.float32)
    table_y[:, : len(ids_q)] = cos_y.T
    table_y[:, wide : wide + len(ids_q)] = sin_y.T
    cos_x, sin_x = waves(ids_p, np.arange(total_x), total_x)
    table_x = np.concatenate((cos_x, sin_x), 0).astype(np.float32)
    pixels = M
    cos_u, sin_u = waves(np.arange(orders_p) - orders_p // 2, np.arange(pixels), pixels)
    strip = pixels // (tiles_x * tiles_y)
    row_table = (np.concatenate((cos_u, sin_u), 0).T / math.sqrt(orders_p)).astype(np.float32)
    row_table = row_table.reshape(tiles_x * tiles_y, strip, 2 * orders_p).astype(jnp.bfloat16)
    cos_v, sin_v = waves(np.arange(orders_q) - orders_q // 2, np.arange(pixels), pixels)
    g_matrix = np.zeros((2 * wide, 2 * pixels), np.float32)
    g_matrix[:orders_q, :pixels] = cos_v / math.sqrt(orders_q)
    g_matrix[:orders_q, pixels:] = sin_v / math.sqrt(orders_q)
    g_matrix[wide : wide + orders_q, :pixels] = -sin_v / math.sqrt(orders_q)
    g_matrix[wide : wide + orders_q, pixels:] = cos_v / math.sqrt(orders_q)
    g_matrix = g_matrix.astype(jnp.bfloat16)

    pieces = [phase] + [cyclic(phase, "gy", by) for by in range(1, tiles_y)]
    part, final = call(
        functools.partial(along_y_kernel, count=tiles_y),
        [(piece, "v") for piece in pieces]
        + [(jnp.asarray(table_y.reshape(tiles_y, lanes, 2 * wide)), "c"), (final, "v")],
        [shape(2 * cells_x, 2 * wide), jax.ShapeDtypeStruct(final.shape, F32)],
        [pltpu.SemaphoreType.DMA],
    )
    parts = [part] + [cyclic(part, "gx", by) for by in range(1, tiles_x)]

    facts = jnp.concatenate([pack[:, orders_p, 0:3] for pack in packs], 0)
    shifts = facts[:, 0:2].astype(jnp.int32)
    weights = facts[:, 2]
    strips = call(
        functools.partial(
            image_kernel,
            tiles_x=tiles_x,
            tiles_y=tiles_y,
            cells_x=cells_x,
            scaling=1.0 / math.sqrt(total_x * total_y * STEPS),
            sources_all=local * tiles_x * tiles_y,
        ),
        [(piece, "v") for piece in parts]
        + [(pack, "v") for pack in packs]
        + [(jnp.asarray(table_x), "c"), (jnp.asarray(g_matrix), "c"), (jnp.asarray(row_table), "c"),
           (shifts, "s"), (weights, "s")],
        [shape(strip, pixels) for _ in range(tiles_x)],
        [
            pltpu.VMEM((2, total_x, 2 * wide), F32),
            pltpu.VMEM((4, reach, wide), F32),
            pltpu.VMEM((2 * orders_p, 4 * pixels), BF16),
            pltpu.VMEM((tiles_x * strip, 2 * orders_p), BF16),
            pltpu.VMEM((tiles_x * strip, pixels), F32),
        ],
    )
    image = strips[0]
    for by in range(1, tiles_x):
        image = image + cyclic(strips[by], "gx", by)
    return (final.reshape(fields.shape), image)


def solution(mesh):
    placed = (
        P("clips", None, "gx", "gy"),
        P("clips", "gx", "gy"),
        P(),
        P(),
        P(("gx", "gy"), None),
        P(("gx", "gy"), None, None),
        P(("gx", "gy")),
    )

    return jax.shard_map(
        body,
        mesh=mesh,
        in_specs=placed,
        out_specs=(P("clips", None, "gx", "gy"), P(("gx", "gy"), "clips")),
        check_vma=False,
    )
```

```python
import functools
import math

import jax
import jax.numpy as jnp
import numpy as np
from jax import lax
from jax.experimental import pallas as pl
from jax.experimental.pallas import tpu as pltpu
from jax.sharding import PartitionSpec as P

STEPS = 12
ROUNDS = 2
M = 512
REACH = 8

COURANT = 0.55
ANGULAR = 0.7
PRECISE = lax.Precision.HIGHEST


F32 = jnp.float32
BF16 = jnp.bfloat16


def vmem():
    return pl.BlockSpec(memory_space=pltpu.VMEM)


def smem():
    return pl.BlockSpec(memory_space=pltpu.SMEM)


def hbm():
    return pl.BlockSpec(memory_space=pltpu.HBM)


def call(kernel, ins, outs, scratch=(), limit=16):
    spaces = {"h": hbm, "c": vmem, "v": vmem, "s": smem}
    memories = {"h": pltpu.HBM, "v": pltpu.VMEM}

    def out_spec(out):
        return vmem() if not isinstance(out, jax.ShapeDtypeStruct) else pl.BlockSpec(memory_space=pl.ANY)

    held = [
        pltpu.with_memory_space_constraint(array, memories[space]) if space in memories else array
        for array, space in ins
    ]
    return pl.pallas_call(
        kernel,
        out_shape=outs,
        in_specs=[spaces[space]() for _, space in ins],
        out_specs=[out_spec(out) for out in outs],
        scratch_shapes=list(scratch),
        compiler_params=pltpu.CompilerParams(vmem_limit_bytes=limit << 20),
    )(*held)


def shape(*dims, dtype=F32):
    return pltpu.VMEM(dims, dtype)


def swap(values, axis, first):
    count = lax.axis_size(axis)
    pairs = []
    for low in range(first, count - 1, 2):
        pairs += [(low, low + 1), (low + 1, low)]
    if not pairs:
        return jnp.zeros_like(values)
    return lax.ppermute(values, axis, pairs)


def cyclic(values, axis, by):
    count = lax.axis_size(axis)
    return lax.ppermute(values, axis, [(i, (i + by) % count) for i in range(count)])


def waves(order_ids, cell_ids, period):
    wrapped = (order_ids[:, None] * cell_ids[None, :]) % period
    angles = 2.0 * math.pi / period * wrapped
    return np.cos(angles), np.sin(angles)


class Geo:
    def __init__(self, depth, cells_x, cells_y, total_x, total_y, count):
        self.depth, self.cells_x, self.cells_y = depth, cells_x, cells_y
        self.total_x, self.total_y, self.count = total_x, total_y, count
        self.wide = 128
        self.per = self.wide // depth
        self.own = cells_x // self.per
        self.groups = 3 * self.own
        self.pad = 16
        self.slack = 8
        self.first = self.slack + self.pad
        self.rows = cells_y + 2 * self.first
        self.half = self.wide // 2
        self.reach = 8
        assert self.per * depth == self.wide and self.own == 2 and cells_x == 2 * self.per
        assert self.per + self.per // 2 == count and STEPS <= self.pad and STEPS - count <= self.reach


PLANES = 6
SCALE = 1.0 / COURANT


def halves_of(planes):
    return (planes + 1) // 2


def pack_rows(get, put, planes, upper, lane, half):
    for plane in range(planes):
        put(plane, get(plane, 1 if upper else 0))
    kept = (lane >= half) if upper else (lane < half)
    group = 0 if upper else 1
    for at in range(halves_of(planes)):
        value = get(2 * at, group)
        if 2 * at + 1 < planes:
            value = jnp.where(kept, value, pltpu.roll(get(2 * at + 1, group), half, 1))
        put(planes + at, value)


def unpack_rows(get, put, planes, inner, outer, kept, half):
    for plane in range(planes):
        put(plane, inner, get(plane))
        value = get(planes + plane // 2)
        if plane % 2:
            value = pltpu.roll(value, half, 1)
        put(plane, outer, jnp.where(kept, value, 0.0))


def pack_kernel(
    far_fields, far_map,
    tile, send_a, send_b, send_c, send_d,
    fields, materials, arrived, *, geo,
):
    copies = [
        pltpu.make_async_copy(far_fields, fields, arrived.at[0]),
        pltpu.make_async_copy(far_map, materials, arrived.at[1]),
    ]
    for copy in copies:
        copy.start()
    for copy in copies:
        copy.wait()
    even_x = lax.axis_index("gx") % 2 == 0
    even_y = lax.axis_index("gy") % 2 == 0
    pad, last = geo.pad, geo.cells_y - geo.pad
    for plane in range(PLANES + 1):
        for group in range(geo.own):
            parts = []
            for x in range(group * geo.per, (group + 1) * geo.per):
                here = pl.ds(x, geo.depth, stride=geo.cells_x)
                parts.append(fields[plane, here, :] if plane < PLANES else materials[here, :].astype(F32))
            values = jnp.concatenate(parts, 0).T
            if 3 <= plane < PLANES:
                values = values * SCALE
            tile[plane, group] = values
            low, high = values[0:pad], values[last:]
            send_c[plane, group] = jnp.where(even_y, high, low)
            send_d[plane, group] = jnp.where(even_y, low, high)
    lane = lax.broadcasted_iota(jnp.int32, (geo.cells_y, geo.wide), 1)

    def fill(send, upper):
        def put(at, value):
            send[at] = value

        pack_rows(lambda plane, group: tile[plane, group], put, PLANES + 1, upper, lane, geo.half)

    @pl.when(even_x)
    def _():
        fill(send_a, True)
        fill(send_b, False)

    @pl.when(jnp.logical_not(even_x))
    def _():
        fill(send_a, False)
        fill(send_b, True)


def source_kernel(masks, shifts, weights, source_pack, square):
    orders_p, orders_q = masks.shape[1:]
    square[...] = jnp.zeros(square.shape, F32)
    source_pack[...] = jnp.zeros(source_pack.shape, F32)
    for source in range(masks.shape[0]):
        square[0:orders_p, 0:orders_q] = masks[source].astype(F32)
        source_pack[source, 0:orders_q, :] = square[...].T[0:orders_q, :]
        for at, fact in enumerate((shifts[0, source], shifts[1, source], weights[source])):
            source_pack[source, orders_q : orders_q + 1, at : at + 1] = jnp.full((1, 1), fact).astype(F32)


def edge_kernel(got_c, got_d, send_a, send_b, *, geo):
    even_x = lax.axis_index("gx") % 2 == 0
    even_y = lax.axis_index("gy") % 2 == 0
    lane = lax.broadcasted_iota(jnp.int32, (geo.pad, geo.wide), 1)

    def fill(send, upper):
        for side in range(2):

            def get(plane, group, side=side):
                c_value, d_value = got_c[plane, group], got_d[plane, group]
                if side:
                    return jnp.where(even_y, c_value, d_value)
                return jnp.where(even_y, d_value, c_value)

            def put(at, value, side=side):
                send[at, side * geo.pad : (side + 1) * geo.pad, :] = value

            pack_rows(get, put, PLANES + 1, upper, lane, geo.half)

    @pl.when(even_x)
    def _():
        fill(send_a, True)
        fill(send_b, False)

    @pl.when(jnp.logical_not(even_x))
    def _():
        fill(send_a, False)
        fill(send_b, True)


def run_steps(state, keep, curl, phase, moments, first_step, geo):
    ex, ey, ez, hx, hy, hz = state
    wide, depth, groups = geo.wide, geo.depth, geo.groups
    first = geo.first
    chunk = 16
    beyond = geo.pad if first_step == 0 else geo.reach
    starts = range(first - beyond, first + geo.cells_y + beyond, chunk)
    lane = lax.broadcasted_iota(jnp.int32, (chunk, wide), 1)
    level = lane % depth
    at_top, at_bottom = level == depth - 1, level == 0
    not_first, not_last = lane >= depth, lane < wide - depth
    low_x = lax.axis_index("gx") == 0
    low_y = lax.axis_index("gy") == 0

    def next_z(values):
        return jnp.where(at_top, 0.0, pltpu.roll(values, wide - 1, 1))

    def last_z(values):
        return jnp.where(at_bottom, 0.0, pltpu.roll(values, 1, 1))

    def magnetic(g, carry):
        after = jnp.minimum(g + 1, groups - 1)
        for start in starts:
            here, ahead = pl.ds(start, chunk), pl.ds(start + 1, chunk)
            x, y, z = ex[g, here, :], ey[g, here, :], ez[g, here, :]
            y_x = pltpu.roll(jnp.where(not_first, y, ey[after, here, :]), wide - depth, 1)
            z_x = pltpu.roll(jnp.where(not_first, z, ez[after, here, :]), wide - depth, 1)
            hx[g, here, :] = hx[g, here, :] - ((ez[g, ahead, :] - z) - (next_z(y) - y))
            hy[g, here, :] = hy[g, here, :] - ((next_z(x) - x) - (z_x - z))
            hz[g, here, :] = hz[g, here, :] - ((y_x - y) - (ex[g, ahead, :] - x))
        return carry

    def electric(g, carry):
        before = jnp.maximum(g - 1, 0)
        for start in starts:
            here, behind = pl.ds(start, chunk), pl.ds(start - 1, chunk)
            x, y, z = hx[g, here, :], hy[g, here, :], hz[g, here, :]
            y_x = pltpu.roll(jnp.where(not_last, y, hy[before, here, :]), depth, 1)
            z_x = pltpu.roll(jnp.where(not_last, z, hz[before, here, :]), depth, 1)
            row = pl.ds(start - first + geo.pad, chunk)
            kept, turned = keep[g, row, :], curl[g, row, :]
            ex[g, here, :] = kept * ex[g, here, :] + turned * ((z - hz[g, behind, :]) - (y - last_z(y)))
            ey[g, here, :] = kept * ey[g, here, :] + turned * ((x - last_z(x)) - (z - z_x))
            ez[g, here, :] = kept * ez[g, here, :] + turned * ((y - y_x) - (x - hx[g, behind, :]))
        return carry

    near = geo.own * geo.per

    def step(index, carry):
        left = geo.count - 1 - index
        low = (near - left - 1) // geo.per
        high = (near + geo.cells_x - 1 + left) // geo.per + 1
        lax.fori_loop(low, high, magnetic, 0)

        @pl.when(low_y)
        def _():
            for field in (hx, hz):
                for g in range(groups):
                    field[g, first - 1 : first, :] = jnp.zeros((1, wide), F32)

        @pl.when(low_x)
        def _():
            for field in (hy, hz):
                for start in starts:
                    here = pl.ds(start, chunk)
                    field[geo.own - 1, here, :] = jnp.where(not_last, field[geo.own - 1, here, :], 0.0)

        lax.fori_loop(low, high, electric, 0)
        at = first_step + index
        cosine, sine = moments[at, 0], moments[at, 1]
        middle = depth // 2
        for start in range(0, geo.cells_y, chunk):
            here = pl.ds(first + start, chunk)
            seen = ex[geo.own, here, :]
            for spot, (field, g) in enumerate(((ex, 1), (ey, 0), (ey, 1)), 1):
                moved = pltpu.roll(field[geo.own + g, here, :], spot, 1)
                seen = jnp.where(level == middle + spot, moved, seen)
            there = pl.ds(start, chunk)
            phase[0, there, :] = phase[0, there, :] + seen * cosine
            phase[1, there, :] = phase[1, there, :] - seen * sine
        return carry

    lax.fori_loop(0, geo.count, step, 0)


def sides(geo):
    odd_x = lax.axis_index("gx") % 2 == 1
    below = (geo.own - 1, geo.own - 2)
    above = (2 * geo.own, 2 * geo.own + 1)
    return [
        (jnp.where(odd_x, below[0], above[0]), jnp.where(odd_x, below[1], above[1]), odd_x),
        (jnp.where(odd_x, above[0], below[0]), jnp.where(odd_x, above[1], below[1]), jnp.logical_not(odd_x)),
    ]


def clear(state, geo, beyond):
    low, high = geo.first - beyond, geo.first + geo.cells_y + beyond
    for field in state:
        for g in range(geo.groups):
            field[g, 0:low, :] = jnp.zeros((low, geo.wide), F32)
            field[g, high : geo.rows, :] = jnp.zeros((geo.rows - high, geo.wide), F32)


def half_lanes(rows, geo, lower):
    lane = lax.broadcasted_iota(jnp.int32, (rows, geo.wide), 1)
    return (lane >= geo.half) == lower


def first_kernel(
    tile, got_a, got_b, got_c, got_d, edge_a, edge_b, tables, moments,
    own, keep, curl, phase, send_a, send_b,
    ex, ey, ez, hx, hy, hz, kinds, *, geo,
):
    state = (ex, ey, ez, hx, hy, hz)
    planes = (*state, kinds)
    even_y = lax.axis_index("gy") % 2 == 0
    pad, first, cells_y = geo.pad, geo.first, geo.cells_y
    main = pl.ds(first, cells_y)
    spans = (pl.ds(first - pad, pad), pl.ds(first + cells_y, pad))
    clear(state, geo, pad)
    for at, plane in enumerate(planes):
        for group in range(geo.own):
            g = geo.own + group
            plane[g, main, :] = tile[at, group]
            c_value, d_value = got_c[at, group], got_d[at, group]
            plane[g, spans[0], :] = jnp.where(even_y, d_value, c_value)
            plane[g, spans[1], :] = jnp.where(even_y, c_value, d_value)
    for got, edge, (inner, outer, lower) in zip((got_a, got_b), (edge_a, edge_b), sides(geo)):

        def put_main(at, g, value):
            planes[at][g, main, :] = value

        unpack_rows(
            lambda at, got=got: got[at], put_main, PLANES + 1, inner, outer, half_lanes(cells_y, geo, lower), geo.half
        )
        for side in range(2):

            def put_side(at, g, value, side=side):
                planes[at][g, spans[side], :] = value

            unpack_rows(
                lambda at, edge=edge, side=side: edge[at, side * pad : (side + 1) * pad, :],
                put_side, PLANES + 1, inner, outer, half_lanes(pad, geo, lower), geo.half,
            )

    chunk = 16
    lane = lax.broadcasted_iota(jnp.int32, (chunk, geo.wide), 1)
    row = lax.broadcasted_iota(jnp.int32, (chunk, geo.wide), 0)
    base_x = (lax.axis_index("gx") - 1) * geo.cells_x
    base_y = lax.axis_index("gy") * cells_y - pad

    def coefs(g, carry):
        place_x = base_x + g * geo.per + lane // geo.depth
        inside_x = (place_x >= 0) & (place_x < geo.total_x)
        for start in range(0, cells_y + 2 * pad, chunk):
            place_y = base_y + start + row
            inside = inside_x & (place_y >= 0) & (place_y < geo.total_y)
            kind = kinds[g, pl.ds(first - pad + start, chunk), :]
            kept = jnp.zeros(kind.shape, F32)
            turned = jnp.zeros(kind.shape, F32)
            for material in range(tables.shape[1]):
                match = kind == float(material)
                kept = jnp.where(match, tables[0, material], kept)
                turned = jnp.where(match, tables[1, material], turned)
            there = pl.ds(start, chunk)
            keep[g, there, :] = jnp.where(inside, kept, 0.0)
            curl[g, there, :] = jnp.where(inside, turned, 0.0)
        return carry

    lax.fori_loop(0, geo.groups, coefs, 0)
    phase[...] = jnp.zeros(phase.shape, F32)
    run_steps(state, keep, curl, phase, moments, 0, geo)

    more = pl.ds(first - geo.reach, cells_y + 2 * geo.reach)
    lane = lax.broadcasted_iota(jnp.int32, (cells_y + 2 * geo.reach, geo.wide), 1)
    for at, field in enumerate(state):
        for group in range(geo.own):
            own[at, group] = field[geo.own + group, more, :]

    def fill(send, upper):
        def put(at, value):
            send[at] = value

        pack_rows(lambda at, group: own[at, group], put, PLANES, upper, lane, geo.half)

    even_x = lax.axis_index("gx") % 2 == 0

    @pl.when(even_x)
    def _():
        fill(send_a, True)
        fill(send_b, False)

    @pl.when(jnp.logical_not(even_x))
    def _():
        fill(send_a, False)
        fill(send_b, True)


def second_kernel(
    own, keep, curl, phase_in, got_a, got_b, moments,
    final, phase,
    ex, ey, ez, hx, hy, hz, seen, *, geo,
):
    state = (ex, ey, ez, hx, hy, hz)
    first, cells_y = geo.first, geo.cells_y
    rows = cells_y + 2 * geo.reach
    more = pl.ds(first - geo.reach, rows)
    clear(state, geo, geo.reach)
    for at, field in enumerate(state):
        for group in range(geo.own):
            field[geo.own + group, more, :] = own[at, group]
    for got, (inner, outer, lower) in zip((got_a, got_b), sides(geo)):

        def put(at, g, value):
            state[at][g, more, :] = value

        unpack_rows(lambda at, got=got: got[at], put, PLANES, inner, outer, half_lanes(rows, geo, lower), geo.half)
    seen[...] = phase_in[...]
    run_steps(state, keep, curl, seen, moments, geo.count, geo)
    middle = geo.depth // 2
    for part in range(2):
        turned = seen[part].T
        for within in range(geo.per):
            for comp in range(2):
                for group in range(geo.own):
                    source = within * geo.depth + middle + comp * geo.own + group
                    target = (part * 2 + comp) * geo.cells_x + group * geo.per + within
                    phase[target : target + 1, :] = turned[source : source + 1, :]
    for at, field in enumerate(state):
        for group in range(geo.own):
            values = field[geo.own + group, pl.ds(first, cells_y), :].T
            if at >= 3:
                values = values * COURANT
            for within in range(geo.per):
                here = pl.ds(group * geo.per + within, geo.depth, stride=geo.cells_x)
                final[at, here, :] = values[within * geo.depth : (within + 1) * geo.depth]


def along_y_kernel(*refs, count):
    pieces, (table, fields, part, kept, done) = refs[:count], refs[count:]
    keeping = pltpu.make_async_copy(fields, kept, done)
    keeping.start()
    me = lax.axis_index("gy")
    total = None
    for back, piece in enumerate(pieces):
        origin = (me - back + count) % count
        term = jnp.dot(piece[...], table[origin], precision=PRECISE, preferred_element_type=F32)
        total = term if total is None else total + term
    rows, width = total.shape[0] // 2, total.shape[1] // 2
    re_cos, re_sin = total[:rows, :width], total[:rows, width:]
    im_cos, im_sin = total[rows:, :width], total[rows:, width:]
    part[:, 0:width] = re_cos + im_sin
    part[:, width : 2 * width] = im_cos - re_sin
    keeping.wait()


def image_kernel(*refs, tiles_x, tiles_y, cells_x, scaling, sources_all):
    parts, refs = refs[:tiles_x], refs[tiles_x:]
    packs, refs = refs[:tiles_y], refs[tiles_y:]
    table_x, g_matrix, row_table, shifts, weights = refs[:5]
    strips, refs = refs[5 : 5 + tiles_x], refs[5 + tiles_x :]
    gathered, orders, rows, turn, spread_a, spread_b, total = refs
    me_x = lax.axis_index("gx")
    me_y = lax.axis_index("gy")
    wide = orders.shape[2]
    for back, part in enumerate(parts):
        origin = pl.multiple_of((me_x - back + tiles_x) % tiles_x * cells_x, cells_x)
        for comp in range(2):
            gathered[comp, pl.ds(origin, cells_x), :] = part[comp * cells_x : (comp + 1) * cells_x, :]
    for comp in range(2):
        re, im = gathered[comp, :, 0:wide], gathered[comp, :, wide : 2 * wide]
        dot = functools.partial(jnp.dot, precision=PRECISE, preferred_element_type=F32)
        cos_x, sin_x = table_x[0:wide, :], table_x[wide : 2 * wide, :]
        order_re = dot(cos_x, re) + dot(sin_x, im)
        order_im = dot(cos_x, im) - dot(sin_x, re)
        orders[2 * comp] = (order_re * scaling).astype(BF16).astype(F32).T
        orders[2 * comp + 1] = (order_im * scaling).astype(BF16).astype(F32).T
    strip = row_table.shape[2]
    mine = tiles_x * strip
    rows[...] = jnp.zeros(rows.shape, F32)
    for ahead in range(tiles_x):
        owner = (me_x + ahead) % tiles_x * tiles_y + me_y
        for part in range(2):
            rows[part, strip * ahead : strip * (ahead + 1), :] = row_table[part, owner]
    cos_u, sin_u = rows[0].T, rows[1].T
    turn[0:wide, 0:wide] = cos_u.astype(BF16)
    turn[0:wide, wide : 2 * wide] = sin_u.astype(BF16)
    turn[wide : 2 * wide, 0:wide] = (-sin_u).astype(BF16)
    turn[wide : 2 * wide, wide : 2 * wide] = cos_u.astype(BF16)
    pixels = g_matrix.shape[0] // 2
    local = packs[0].shape[0]
    orders_q = packs[0].shape[1] - 8
    count = local * tiles_y

    def spread(number, pack, index, out):
        down = shifts[number, 1] + REACH
        across = wide - (shifts[number, 0] + REACH)
        passed = pack[index, 0:orders_q, :]
        masked = []
        for plane in range(4):
            window = orders[plane, pl.ds(down, orders_q), :]
            value = pltpu.roll(window, across, 1) * passed
            masked.append(jnp.concatenate((value, jnp.zeros((wide - orders_q, wide), F32)), 0).astype(BF16))
        halves = jnp.concatenate(
            (jnp.concatenate((masked[0], masked[2]), 1), jnp.concatenate((masked[1], masked[3]), 1)), 0
        )
        both = jnp.dot(g_matrix[...], halves, preferred_element_type=F32).astype(BF16)
        for comp in range(2):
            low = 2 * comp * wide
            out[:, low : low + wide] = both[0:pixels, comp * wide : (comp + 1) * wide]
            out[:, low + wide : low + 2 * wide] = both[pixels:, comp * wide : (comp + 1) * wide]

    def expose(number, made):
        bright = None
        for comp in range(2):
            low = 2 * comp * wide
            value = jnp.dot(made[:, low : low + 2 * wide], turn[...], preferred_element_type=F32)
            value = value * value
            value = value[:, 0:wide] + value[:, wide : 2 * wide]
            bright = value if bright is None else bright + value
        total[...] = total[...] + (weights[number] / sources_all) * bright

    total[...] = jnp.zeros(total.shape, F32)
    slots = (spread_a, spread_b)
    spread(0, packs[0], 0, slots[0])
    for at, pack in enumerate(packs):
        following = packs[min(at + 1, tiles_y - 1)]
        for index in range(local):
            number = at * local + index
            if number + 1 < count:
                last = index + 1 == local
                spread(number + 1, following if last else pack, 0 if last else index + 1, slots[(number + 1) % 2])
            expose(number, slots[number % 2])
    for block in range(pixels // wide):
        turned = total[block * wide : (block + 1) * wide, :].T
        for ahead in range(tiles_x):
            strips[ahead][:, block * wide : (block + 1) * wide] = turned[strip * ahead : strip * (ahead + 1), :]
    assert mine <= wide


def body(
    fields, material_map, material_eps, material_loss, source_shift, source_mask, source_weight
):
    tiles_x = lax.axis_size("gx")
    tiles_y = lax.axis_size("gy")
    _, depth, cells_x, lanes = fields.shape
    total_x, total_y = cells_x * tiles_x, lanes * tiles_y
    count = STEPS // ROUNDS
    geo = Geo(depth, cells_x, lanes, total_x, total_y, count)
    flat_fields = fields.reshape(6, depth * cells_x, lanes)
    flat_map = material_map.reshape(depth * cells_x, lanes)
    local, orders_p, orders_q = source_mask.shape
    wide = 128

    keep_table = (1.0 - material_loss) / (1.0 + material_loss)
    curl_table = COURANT * (COURANT / (material_eps * (1.0 + material_loss)))
    tables = jnp.stack((keep_table, curl_table))
    angle = np.float32(ANGULAR) * np.arange(1, STEPS + 1, dtype=np.float32)
    moments = jnp.asarray(np.stack((np.cos(angle), np.sin(angle)), 1).astype(np.float32))

    sent = PLANES + 1 + halves_of(PLANES + 1)
    row_shape = shape(sent, lanes, wide)
    side_shape = shape(PLANES + 1, geo.own, geo.pad, wide)
    edge_shape = shape(sent, 2 * geo.pad, wide)
    tile, to_a, to_b, to_c, to_d = call(
        functools.partial(pack_kernel, geo=geo),
        [(flat_fields, "h"), (flat_map, "h")],
        [shape(PLANES + 1, geo.own, lanes, wide), row_shape, row_shape, side_shape, side_shape],
        [
            pltpu.VMEM(flat_fields.shape, F32),
            pltpu.VMEM(flat_map.shape, jnp.int32),
            pltpu.SemaphoreType.DMA((2,)),
        ],
    )
    got_c = swap(to_c, "gy", 0)
    got_d = swap(to_d, "gy", 1)
    got_a = swap(to_a, "gx", 0)
    got_b = swap(to_b, "gx", 1)
    to_a, to_b = call(functools.partial(edge_kernel, geo=geo), [(got_c, "v"), (got_d, "v")], [edge_shape, edge_shape])
    edge_a = swap(to_a, "gx", 0)
    edge_b = swap(to_b, "gx", 1)
    (my_pack,) = call(
        source_kernel,
        [(source_mask, "c"), (source_shift.T, "s"), (source_weight, "s")],
        [shape(local, orders_q + 8, wide)],
        [pltpu.VMEM((wide, wide), F32)],
    )
    packs = [my_pack]
    for by in range(1, tiles_y):
        packs.append(cyclic(my_pack, "gy", by))

    state = [pltpu.VMEM((geo.groups, geo.rows, wide), F32) for _ in range(PLANES)]
    coef_shape = shape(geo.groups, lanes + 2 * geo.pad, wide)
    seen_shape = shape(2, lanes, wide)
    longer = lanes + 2 * geo.reach
    send_shape = shape(PLANES + halves_of(PLANES), longer, wide)
    own, keep, curl, seen, to_a, to_b = call(
        functools.partial(first_kernel, geo=geo),
        [(tile, "v"), (got_a, "v"), (got_b, "v"), (got_c, "v"), (got_d, "v"), (edge_a, "v"), (edge_b, "v"),
         (tables, "s"), (moments, "s")],
        [shape(PLANES, geo.own, longer, wide), coef_shape, coef_shape, seen_shape, send_shape, send_shape],
        [*state, pltpu.VMEM((geo.groups, geo.rows, wide), F32)],
    )
    got_a = swap(to_a, "gx", 0)
    got_b = swap(to_b, "gx", 1)
    final, phase = call(
        functools.partial(second_kernel, geo=geo),
        [(own, "v"), (keep, "v"), (curl, "v"), (seen, "v"), (got_a, "v"), (got_b, "v"), (moments, "s")],
        [shape(PLANES, depth * cells_x, lanes), shape(4 * cells_x, lanes)],
        [*state, pltpu.VMEM((2, lanes, wide), F32)],
    )

    ids_p = np.arange(-REACH, wide - REACH) % orders_p - orders_p // 2
    ids_q = np.arange(-REACH, wide - REACH) % orders_q - orders_q // 2
    cos_y, sin_y = waves(ids_q, np.arange(total_y), total_y)
    table_y = np.zeros((total_y, 2 * wide), np.float32)
    table_y[:, : len(ids_q)] = cos_y.T
    table_y[:, wide : wide + len(ids_q)] = sin_y.T
    cos_x, sin_x = waves(ids_p, np.arange(total_x), total_x)
    table_x = np.concatenate((cos_x, sin_x), 0).astype(np.float32)
    pixels = M
    cos_u, sin_u = waves(np.arange(orders_p) - orders_p // 2, np.arange(pixels), pixels)
    strip = pixels // (tiles_x * tiles_y)
    row_table = np.zeros((2, tiles_x * tiles_y, strip, wide), np.float32)
    row_table[0, :, :, :orders_p] = (cos_u.T / math.sqrt(orders_p)).reshape(-1, strip, orders_p)
    row_table[1, :, :, :orders_p] = (sin_u.T / math.sqrt(orders_p)).reshape(-1, strip, orders_p)
    cos_v, sin_v = waves(np.arange(orders_q) - orders_q // 2, np.arange(pixels), pixels)
    g_matrix = np.zeros((2 * pixels, 2 * wide), np.float32)
    g_matrix[:pixels, :orders_q] = cos_v.T / math.sqrt(orders_q)
    g_matrix[pixels:, :orders_q] = sin_v.T / math.sqrt(orders_q)
    g_matrix[:pixels, wide : wide + orders_q] = -sin_v.T / math.sqrt(orders_q)
    g_matrix[pixels:, wide : wide + orders_q] = cos_v.T / math.sqrt(orders_q)
    g_matrix = g_matrix.astype(jnp.bfloat16)

    pieces = [phase] + [cyclic(phase, "gy", by) for by in range(1, tiles_y)]
    part, final = call(
        functools.partial(along_y_kernel, count=tiles_y),
        [(piece, "v") for piece in pieces]
        + [(jnp.asarray(table_y.reshape(tiles_y, lanes, 2 * wide)), "c"), (final, "v")],
        [shape(2 * cells_x, 2 * wide), jax.ShapeDtypeStruct(final.shape, F32)],
        [pltpu.SemaphoreType.DMA],
    )
    parts = [part] + [cyclic(part, "gx", by) for by in range(1, tiles_x)]

    facts = jnp.concatenate([pack[:, orders_q, 0:3] for pack in packs], 0)
    shifts = facts[:, 0:2].astype(jnp.int32)
    weights = facts[:, 2]
    strips = call(
        functools.partial(
            image_kernel,
            tiles_x=tiles_x,
            tiles_y=tiles_y,
            cells_x=cells_x,
            scaling=1.0 / math.sqrt(total_x * total_y * STEPS),
            sources_all=local * tiles_x * tiles_y,
        ),
        [(piece, "v") for piece in parts]
        + [(pack, "v") for pack in packs]
        + [(jnp.asarray(table_x), "c"), (jnp.asarray(g_matrix), "c"), (jnp.asarray(row_table), "c"),
           (shifts, "s"), (weights, "s")],
        [shape(strip, pixels) for _ in range(tiles_x)],
        [
            pltpu.VMEM((2, total_x, 2 * wide), F32),
            pltpu.VMEM((4, wide, wide), F32),
            pltpu.VMEM((2, wide, wide), F32),
            pltpu.VMEM((2 * wide, 2 * wide), BF16),
            pltpu.VMEM((pixels, 4 * wide), BF16),
            pltpu.VMEM((pixels, 4 * wide), BF16),
            pltpu.VMEM((pixels, wide), F32),
        ],
    )
    image = strips[0]
    for by in range(1, tiles_x):
        image = image + cyclic(strips[by], "gx", by)
    return (final.reshape(fields.shape), image)


def solution(mesh):
    placed = (
        P("clips", None, "gx", "gy"),
        P("clips", "gx", "gy"),
        P(),
        P(),
        P(("gx", "gy"), None),
        P(("gx", "gy"), None, None),
        P(("gx", "gy")),
    )

    return jax.shard_map(
        body,
        mesh=mesh,
        in_specs=placed,
        out_specs=(P("clips", None, "gx", "gy"), P(("gx", "gy"), "clips")),
        check_vma=False,
    )
```

```python
import functools
import math

import jax
import jax.numpy as jnp
import numpy as np
from jax import lax
from jax.experimental import pallas as pl
from jax.experimental.pallas import tpu as pltpu
from jax.sharding import PartitionSpec as P

STEPS = 12
M = 512
REACH = 8

COURANT = 0.55
ANGULAR = 0.7
PRECISE = lax.Precision.HIGHEST


F32 = jnp.float32
BF16 = jnp.bfloat16


def vmem():
    return pl.BlockSpec(memory_space=pltpu.VMEM)


def smem():
    return pl.BlockSpec(memory_space=pltpu.SMEM)


def hbm():
    return pl.BlockSpec(memory_space=pltpu.HBM)


def call(kernel, ins, outs, scratch=(), limit=16):
    spaces = {"h": hbm, "c": vmem, "v": vmem, "s": smem}
    memories = {"h": pltpu.HBM, "v": pltpu.VMEM}

    def out_spec(out):
        return vmem() if not isinstance(out, jax.ShapeDtypeStruct) else pl.BlockSpec(memory_space=pl.ANY)

    held = [
        pltpu.with_memory_space_constraint(array, memories[space]) if space in memories else array
        for array, space in ins
    ]
    return pl.pallas_call(
        kernel,
        out_shape=outs,
        in_specs=[spaces[space]() for _, space in ins],
        out_specs=[out_spec(out) for out in outs],
        scratch_shapes=list(scratch),
        compiler_params=pltpu.CompilerParams(vmem_limit_bytes=limit << 20),
    )(*held)


def shape(*dims, dtype=F32):
    return pltpu.VMEM(dims, dtype)


def swap(values, axis, first):
    count = lax.axis_size(axis)
    pairs = []
    for low in range(first, count - 1, 2):
        pairs += [(low, low + 1), (low + 1, low)]
    if not pairs:
        return jnp.zeros_like(values)
    return lax.ppermute(values, axis, pairs)


def cyclic(values, axis, by):
    count = lax.axis_size(axis)
    return lax.ppermute(values, axis, [(i, (i + by) % count) for i in range(count)])


def waves(order_ids, cell_ids, period):
    wrapped = (order_ids[:, None] * cell_ids[None, :]) % period
    angles = 2.0 * math.pi / period * wrapped
    return np.cos(angles), np.sin(angles)


class Geo:
    def __init__(self, depth, cells_x, cells_y, total_x, total_y):
        self.depth, self.cells_x, self.cells_y = depth, cells_x, cells_y
        self.total_x, self.total_y = total_x, total_y
        self.wide = 128
        self.per = self.wide // depth
        self.own = cells_x // self.per
        self.groups = 3 * self.own
        self.pad = 16
        self.slack = 8
        self.first = self.slack + self.pad
        self.rows = cells_y + 2 * self.first
        self.reach = 8
        self.counts = (min(cells_x, STEPS), max(STEPS - cells_x, 0))
        assert self.per * depth == self.wide and self.own == 2 and cells_x == 2 * self.per
        assert self.counts[1] <= min(self.per, self.reach) and STEPS <= self.pad

    def plane(self):
        return pltpu.VMEM(((self.groups + 4) * self.rows, self.wide), F32)

    def at(self, group, row, count):
        return pl.ds(pl.multiple_of((group + 2) * self.rows, 8) + row, count)


PLANES = 6
SCALE = 1.0 / COURANT


def pack_kernel(
    far_fields, far_map,
    tile, send_c, send_d,
    fields, materials, arrived, *, geo,
):
    copies = [
        pltpu.make_async_copy(far_fields, fields, arrived.at[0]),
        pltpu.make_async_copy(far_map, materials, arrived.at[1]),
    ]
    for copy in copies:
        copy.start()
    for copy in copies:
        copy.wait()
    even_y = lax.axis_index("gy") % 2 == 0
    pad, last = geo.pad, geo.cells_y - geo.pad
    for plane in range(PLANES + 1):
        for group in range(geo.own):
            parts = []
            for x in range(group * geo.per, (group + 1) * geo.per):
                here = pl.ds(x, geo.depth, stride=geo.cells_x)
                parts.append(fields[plane, here, :] if plane < PLANES else materials[here, :].astype(F32))
            values = jnp.concatenate(parts, 0).T
            if 3 <= plane < PLANES:
                values = values * SCALE
            tile[plane, group] = values
            low, high = values[0:pad], values[last:]
            send_c[plane, group] = jnp.where(even_y, high, low)
            send_d[plane, group] = jnp.where(even_y, low, high)


def source_kernel(masks, shifts, weights, source_pack, square):
    orders_p, orders_q = masks.shape[1:]
    square[...] = jnp.zeros(square.shape, F32)
    source_pack[...] = jnp.zeros(source_pack.shape, F32)
    for source in range(masks.shape[0]):
        square[0:orders_p, 0:orders_q] = masks[source].astype(F32)
        source_pack[source, 0:orders_q, :] = square[...].T[0:orders_q, :]
        for at, fact in enumerate((shifts[0, source], shifts[1, source], weights[source])):
            source_pack[source, orders_q : orders_q + 1, at : at + 1] = jnp.full((1, 1), fact).astype(F32)


def edge_kernel(got_c, got_d, edges, *, geo):
    even_y = lax.axis_index("gy") % 2 == 0
    for plane in range(PLANES + 1):
        for group in range(geo.own):
            c_value, d_value = got_c[plane, group], got_d[plane, group]
            edges[plane, group, 0 : geo.pad] = jnp.where(even_y, d_value, c_value)
            edges[plane, group, geo.pad : 2 * geo.pad] = jnp.where(even_y, c_value, d_value)


def run_steps(state, keep, curl, phase, moments, first_step, count, beyond, geo):
    ex, ey, _, _, hy, hz = state
    wide, depth, rows = geo.wide, geo.depth, geo.rows
    first = geo.first
    chunk = 16
    starts = range(first - beyond, first + geo.cells_y + beyond, chunk)
    lane = lax.broadcasted_iota(jnp.int32, (chunk, wide), 1)
    row = lax.broadcasted_iota(jnp.int32, (chunk, wide), 0)
    level = lane % depth
    at_top, at_bottom = level == depth - 1, level == 0
    not_first, not_last = lane >= depth, lane < wide - depth
    low_x = lax.axis_index("gx") == 0
    open_y = jnp.where(lax.axis_index("gy") == 0, 0.0, 1.0)

    def next_z(values):
        return jnp.where(at_top, 0.0, pltpu.roll(values, wide - 1, 1))

    def last_z(values):
        return jnp.where(at_bottom, 0.0, pltpu.roll(values, 1, 1))

    def gated(values, start):
        if start <= first - 1 < start + chunk:
            return values * jnp.where(row == first - 1 - start, open_y, 1.0)
        return values

    def magnetic(g, carry):
        base = pl.multiple_of((g + 2) * rows, 8)
        ex, ey, ez, hx, hy, hz = [field.at[pl.ds(base, 2 * rows), :] for field in state]
        for start in starts:
            here, ahead = pl.ds(start, chunk), pl.ds(start + 1, chunk)
            over = pl.ds(rows + start, chunk)
            x, y, z = ex[here, :], ey[here, :], ez[here, :]
            y_x = pltpu.roll(jnp.where(not_first, y, ey[over, :]), wide - depth, 1)
            z_x = pltpu.roll(jnp.where(not_first, z, ez[over, :]), wide - depth, 1)
            hx[here, :] = gated(hx[here, :] - ((ez[ahead, :] - z) - (next_z(y) - y)), start)
            hy[here, :] = hy[here, :] - ((next_z(x) - x) - (z_x - z))
            hz[here, :] = gated(hz[here, :] - ((y_x - y) - (ex[ahead, :] - x)), start)
        return carry

    def electric(g, carry):
        base = pl.multiple_of((g + 1) * rows, 8)
        ex, ey, ez, hx, hy, hz = [field.at[pl.ds(base, 2 * rows), :] for field in state]
        kept_all, turned_all = keep.at[g], curl.at[g]
        for start in starts:
            here, behind = pl.ds(rows + start, chunk), pl.ds(rows + start - 1, chunk)
            under = pl.ds(start, chunk)
            x, y, z = hx[here, :], hy[here, :], hz[here, :]
            y_x = pltpu.roll(jnp.where(not_last, y, hy[under, :]), depth, 1)
            z_x = pltpu.roll(jnp.where(not_last, z, hz[under, :]), depth, 1)
            spot = pl.ds(start - first + geo.pad, chunk)
            kept, turned = kept_all[spot, :], turned_all[spot, :]
            ex[here, :] = kept * ex[here, :] + turned * ((z - hz[behind, :]) - (y - last_z(y)))
            ey[here, :] = kept * ey[here, :] + turned * ((x - last_z(x)) - (z - z_x))
            ez[here, :] = kept * ez[here, :] + turned * ((y - y_x) - (x - hx[behind, :]))
        return carry

    near = geo.own * geo.per

    def step(index, carry):
        left = count - 1 - index
        low = (near - left - 1) // geo.per
        high = (near + geo.cells_x - 1 + left) // geo.per
        lax.fori_loop(low, high + 1, magnetic, 0)

        @pl.when(low_x)
        def _():
            for field in (hy, hz):
                field[geo.at(geo.own - 1, 0, rows), :] = jnp.zeros((rows, wide), F32)

        lax.fori_loop(low, high + 1, electric, 0)
        at = first_step + index
        cosine, sine = moments[at, 0], moments[at, 1]
        middle = depth // 2
        for start in range(0, geo.cells_y, chunk):
            seen = ex[geo.at(geo.own, first + start, chunk), :]
            for spot, (field, g) in enumerate(((ex, 1), (ey, 0), (ey, 1)), 1):
                moved = pltpu.roll(field[geo.at(geo.own + g, first + start, chunk), :], spot, 1)
                seen = jnp.where(level == middle + spot, moved, seen)
            there = pl.ds(start, chunk)
            phase[0, there, :] = phase[0, there, :] + seen * cosine
            phase[1, there, :] = phase[1, there, :] - seen * sine
        return carry

    lax.fori_loop(0, count, step, 0)


def clear(state, geo, beyond):
    low, high = geo.first - beyond, geo.first + geo.cells_y + beyond
    for field in state:
        for g in (-2, -1, geo.groups, geo.groups + 1):
            field[geo.at(g, 0, geo.rows), :] = jnp.zeros((geo.rows, geo.wide), F32)
        for g in range(geo.groups):
            field[geo.at(g, 0, low), :] = jnp.zeros((low, geo.wide), F32)
            field[geo.at(g, high, geo.rows - high), :] = jnp.zeros((geo.rows - high, geo.wide), F32)


def first_kernel(
    tile, got_a, got_b, got_c, got_d, edge_a, edge_b, tables, moments,
    own, keep, curl, phase, send_a, send_b,
    ex, ey, ez, hx, hy, hz, kinds, *, geo,
):
    state = (ex, ey, ez, hx, hy, hz)
    planes = (*state, kinds)
    even_y = lax.axis_index("gy") % 2 == 0
    odd_x = lax.axis_index("gx") % 2 == 1
    pad, first, cells_y = geo.pad, geo.first, geo.cells_y
    clear(state, geo, pad)
    base_a = jnp.where(odd_x, 0, 2 * geo.own)
    base_b = jnp.where(odd_x, 2 * geo.own, 0)
    for at, plane in enumerate(planes):
        for group in range(geo.own):
            g = geo.own + group
            plane[geo.at(g, first, cells_y), :] = tile[at, group]
            c_value, d_value = got_c[at, group], got_d[at, group]
            plane[geo.at(g, first - pad, pad), :] = jnp.where(even_y, d_value, c_value)
            plane[geo.at(g, first + cells_y, pad), :] = jnp.where(even_y, c_value, d_value)
            for got, edge, base in ((got_a, edge_a, base_a), (got_b, edge_b, base_b)):
                plane[geo.at(base + group, first, cells_y), :] = got[at, group]
                plane[geo.at(base + group, first - pad, pad), :] = edge[at, group, 0:pad]
                plane[geo.at(base + group, first + cells_y, pad), :] = edge[at, group, pad : 2 * pad]

    chunk = 16
    lane = lax.broadcasted_iota(jnp.int32, (chunk, geo.wide), 1)
    row = lax.broadcasted_iota(jnp.int32, (chunk, geo.wide), 0)
    base_x = (lax.axis_index("gx") - 1) * geo.cells_x
    base_y = lax.axis_index("gy") * cells_y - pad

    def coefs(g, carry):
        place_x = base_x + g * geo.per + lane // geo.depth
        inside_x = (place_x >= 0) & (place_x < geo.total_x)
        for start in range(0, cells_y + 2 * pad, chunk):
            place_y = base_y + start + row
            inside = inside_x & (place_y >= 0) & (place_y < geo.total_y)
            kind = kinds[geo.at(g, first - pad + start, chunk), :]
            kept = jnp.zeros(kind.shape, F32)
            turned = jnp.zeros(kind.shape, F32)
            for material in range(tables.shape[1]):
                match = kind == float(material)
                kept = jnp.where(match, tables[0, material], kept)
                turned = jnp.where(match, tables[1, material], turned)
            there = pl.ds(start, chunk)
            keep[g, there, :] = jnp.where(inside, kept, 0.0)
            curl[g, there, :] = jnp.where(inside, turned, 0.0)
        return carry

    lax.fori_loop(0, geo.groups, coefs, 0)
    phase[...] = jnp.zeros(phase.shape, F32)
    run_steps(state, keep, curl, phase, moments, 0, geo.counts[0], pad, geo)

    rows = cells_y + 2 * geo.reach
    near_a = jnp.where(odd_x, 0, geo.own - 1)
    near_b = jnp.where(odd_x, geo.own - 1, 0)
    for at, field in enumerate(state):
        for group in range(geo.own):
            own[at, group] = field[geo.at(geo.own + group, first - geo.reach, rows), :]
        send_a[at] = field[geo.at(geo.own + near_a, first - geo.reach, rows), :]
        send_b[at] = field[geo.at(geo.own + near_b, first - geo.reach, rows), :]


def second_kernel(
    own, keep, curl, phase_in, got_a, got_b, moments,
    final, phase,
    ex, ey, ez, hx, hy, hz, seen, *, geo,
):
    state = (ex, ey, ez, hx, hy, hz)
    first, cells_y, reach = geo.first, geo.cells_y, geo.reach
    rows = cells_y + 2 * reach
    odd_x = lax.axis_index("gx") % 2 == 1
    clear(state, geo, reach)
    below, above = geo.own - 1, 2 * geo.own
    base_a = jnp.where(odd_x, below, above)
    base_b = jnp.where(odd_x, above, below)
    for at, field in enumerate(state):
        for g in (below - 1, above + 1):
            field[geo.at(g, first - reach, rows), :] = jnp.zeros((rows, geo.wide), F32)
        for group in range(geo.own):
            field[geo.at(geo.own + group, first - reach, rows), :] = own[at, group]
        field[geo.at(base_a, first - reach, rows), :] = got_a[at]
        field[geo.at(base_b, first - reach, rows), :] = got_b[at]
    seen[...] = phase_in[...]
    run_steps(state, keep, curl, seen, moments, geo.counts[0], geo.counts[1], reach, geo)
    middle = geo.depth // 2
    for part in range(2):
        turned = seen[part].T
        for within in range(geo.per):
            for comp in range(2):
                for group in range(geo.own):
                    source = within * geo.depth + middle + comp * geo.own + group
                    target = (part * 2 + comp) * geo.cells_x + group * geo.per + within
                    phase[target : target + 1, :] = turned[source : source + 1, :]
    for at, field in enumerate(state):
        for group in range(geo.own):
            values = field[geo.at(geo.own + group, first, cells_y), :].T
            if at >= 3:
                values = values * COURANT
            for within in range(geo.per):
                here = pl.ds(group * geo.per + within, geo.depth, stride=geo.cells_x)
                final[at, here, :] = values[within * geo.depth : (within + 1) * geo.depth]


def along_y_kernel(*refs, count):
    pieces, (table, fields, part, kept, done) = refs[:count], refs[count:]
    keeping = pltpu.make_async_copy(fields, kept, done)
    keeping.start()
    me = lax.axis_index("gy")
    total = None
    for back, piece in enumerate(pieces):
        origin = (me - back + count) % count
        term = jnp.dot(piece[...], table[origin], precision=PRECISE, preferred_element_type=F32)
        total = term if total is None else total + term
    rows, width = total.shape[0] // 2, total.shape[1] // 2
    re_cos, re_sin = total[:rows, :width], total[:rows, width:]
    im_cos, im_sin = total[rows:, :width], total[rows:, width:]
    part[:, 0:width] = re_cos + im_sin
    part[:, width : 2 * width] = im_cos - re_sin
    keeping.wait()


def image_kernel(*refs, tiles_x, tiles_y, cells_x, scaling, sources_all):
    parts, refs = refs[:tiles_x], refs[tiles_x:]
    packs, refs = refs[:tiles_y], refs[tiles_y:]
    table_x, g_matrix, row_table, shifts, weights = refs[:5]
    strips, refs = refs[5 : 5 + tiles_x], refs[5 + tiles_x :]
    gathered, orders, rows, turn, spread_a, spread_b, total = refs
    me_x = lax.axis_index("gx")
    me_y = lax.axis_index("gy")
    wide = orders.shape[2]
    for back, part in enumerate(parts):
        origin = pl.multiple_of((me_x - back + tiles_x) % tiles_x * cells_x, cells_x)
        for comp in range(2):
            gathered[comp, pl.ds(origin, cells_x), :] = part[comp * cells_x : (comp + 1) * cells_x, :]
    for comp in range(2):
        re, im = gathered[comp, :, 0:wide], gathered[comp, :, wide : 2 * wide]
        dot = functools.partial(jnp.dot, precision=PRECISE, preferred_element_type=F32)
        cos_x, sin_x = table_x[0:wide, :], table_x[wide : 2 * wide, :]
        order_re = dot(cos_x, re) + dot(sin_x, im)
        order_im = dot(cos_x, im) - dot(sin_x, re)
        orders[2 * comp] = (order_re * scaling).astype(BF16).astype(F32).T
        orders[2 * comp + 1] = (order_im * scaling).astype(BF16).astype(F32).T
    strip = row_table.shape[2]
    mine = tiles_x * strip
    rows[...] = jnp.zeros(rows.shape, F32)
    for ahead in range(tiles_x):
        owner = (me_x + ahead) % tiles_x * tiles_y + me_y
        for part in range(2):
            rows[part, strip * ahead : strip * (ahead + 1), :] = row_table[part, owner]
    cos_u, sin_u = rows[0].T, rows[1].T
    turn[0:wide, 0:wide] = cos_u.astype(BF16)
    turn[0:wide, wide : 2 * wide] = sin_u.astype(BF16)
    turn[wide : 2 * wide, 0:wide] = (-sin_u).astype(BF16)
    turn[wide : 2 * wide, wide : 2 * wide] = cos_u.astype(BF16)
    pixels = g_matrix.shape[0] // 2
    local = packs[0].shape[0]
    orders_q = packs[0].shape[1] - 8
    count = local * tiles_y

    def spread(number, pack, index, out):
        down = shifts[number, 1] + REACH
        across = wide - (shifts[number, 0] + REACH)
        passed = pack[index, 0:orders_q, :]
        masked = []
        for plane in range(4):
            window = orders[plane, pl.ds(down, orders_q), :]
            value = pltpu.roll(window, across, 1) * passed
            masked.append(jnp.concatenate((value, jnp.zeros((wide - orders_q, wide), F32)), 0).astype(BF16))
        halves = jnp.concatenate(
            (jnp.concatenate((masked[0], masked[2]), 1), jnp.concatenate((masked[1], masked[3]), 1)), 0
        )
        both = jnp.dot(g_matrix[...], halves, preferred_element_type=F32).astype(BF16)
        for comp in range(2):
            low = 2 * comp * wide
            out[:, low : low + wide] = both[0:pixels, comp * wide : (comp + 1) * wide]
            out[:, low + wide : low + 2 * wide] = both[pixels:, comp * wide : (comp + 1) * wide]

    def expose(number, made):
        bright = None
        for comp in range(2):
            low = 2 * comp * wide
            value = jnp.dot(made[:, low : low + 2 * wide], turn[...], preferred_element_type=F32)
            value = value * value
            value = value[:, 0:wide] + value[:, wide : 2 * wide]
            bright = value if bright is None else bright + value
        total[...] = total[...] + (weights[number] / sources_all) * bright

    total[...] = jnp.zeros(total.shape, F32)
    slots = (spread_a, spread_b)
    spread(0, packs[0], 0, slots[0])
    for at, pack in enumerate(packs):
        following = packs[min(at + 1, tiles_y - 1)]
        for index in range(local):
            number = at * local + index
            if number + 1 < count:
                last = index + 1 == local
                spread(number + 1, following if last else pack, 0 if last else index + 1, slots[(number + 1) % 2])
            expose(number, slots[number % 2])
    for block in range(pixels // wide):
        turned = total[block * wide : (block + 1) * wide, :].T
        for ahead in range(tiles_x):
            strips[ahead][:, block * wide : (block + 1) * wide] = turned[strip * ahead : strip * (ahead + 1), :]
    assert mine <= wide


def body(
    fields, material_map, material_eps, material_loss, source_shift, source_mask, source_weight
):
    tiles_x = lax.axis_size("gx")
    tiles_y = lax.axis_size("gy")
    _, depth, cells_x, lanes = fields.shape
    total_x, total_y = cells_x * tiles_x, lanes * tiles_y
    geo = Geo(depth, cells_x, lanes, total_x, total_y)
    flat_fields = fields.reshape(6, depth * cells_x, lanes)
    flat_map = material_map.reshape(depth * cells_x, lanes)
    local, orders_p, orders_q = source_mask.shape
    wide = 128

    keep_table = (1.0 - material_loss) / (1.0 + material_loss)
    curl_table = COURANT * (COURANT / (material_eps * (1.0 + material_loss)))
    tables = jnp.stack((keep_table, curl_table))
    angle = np.float32(ANGULAR) * np.arange(1, STEPS + 1, dtype=np.float32)
    moments = jnp.asarray(np.stack((np.cos(angle), np.sin(angle)), 1).astype(np.float32))

    side_shape = shape(PLANES + 1, geo.own, geo.pad, wide)
    tile, to_c, to_d = call(
        functools.partial(pack_kernel, geo=geo),
        [(flat_fields, "h"), (flat_map, "h")],
        [shape(PLANES + 1, geo.own, lanes, wide), side_shape, side_shape],
        [
            pltpu.VMEM(flat_fields.shape, F32),
            pltpu.VMEM(flat_map.shape, jnp.int32),
            pltpu.SemaphoreType.DMA((2,)),
        ],
    )
    got_c = swap(to_c, "gy", 0)
    got_d = swap(to_d, "gy", 1)
    got_a = swap(tile, "gx", 0)
    got_b = swap(tile, "gx", 1)
    (edges,) = call(
        functools.partial(edge_kernel, geo=geo),
        [(got_c, "v"), (got_d, "v")],
        [shape(PLANES + 1, geo.own, 2 * geo.pad, wide)],
    )
    edge_a = swap(edges, "gx", 0)
    edge_b = swap(edges, "gx", 1)

    state = [geo.plane() for _ in range(PLANES)]
    coef_shape = shape(geo.groups, lanes + 2 * geo.pad, wide)
    seen_shape = shape(2, lanes, wide)
    longer = lanes + 2 * geo.reach
    send_shape = shape(PLANES, longer, wide)
    own, keep, curl, seen, to_a, to_b = call(
        functools.partial(first_kernel, geo=geo),
        [(tile, "v"), (got_a, "v"), (got_b, "v"), (got_c, "v"), (got_d, "v"), (edge_a, "v"), (edge_b, "v"),
         (tables, "s"), (moments, "s")],
        [shape(PLANES, geo.own, longer, wide), coef_shape, coef_shape, seen_shape, send_shape, send_shape],
        [*state, geo.plane()],
    )
    got_a = swap(to_a, "gx", 0)
    got_b = swap(to_b, "gx", 1)
    (my_pack,) = call(
        source_kernel,
        [(source_mask, "c"), (source_shift.T, "s"), (source_weight, "s")],
        [shape(local, orders_q + 8, wide)],
        [pltpu.VMEM((wide, wide), F32)],
    )
    packs = [my_pack]
    for by in range(1, tiles_y):
        packs.append(cyclic(my_pack, "gy", by))
    final, phase = call(
        functools.partial(second_kernel, geo=geo),
        [(own, "v"), (keep, "v"), (curl, "v"), (seen, "v"), (got_a, "v"), (got_b, "v"), (moments, "s")],
        [shape(PLANES, depth * cells_x, lanes), shape(4 * cells_x, lanes)],
        [*state, pltpu.VMEM((2, lanes, wide), F32)],
    )

    ids_p = np.arange(-REACH, wide - REACH) % orders_p - orders_p // 2
    ids_q = np.arange(-REACH, wide - REACH) % orders_q - orders_q // 2
    cos_y, sin_y = waves(ids_q, np.arange(total_y), total_y)
    table_y = np.zeros((total_y, 2 * wide), np.float32)
    table_y[:, : len(ids_q)] = cos_y.T
    table_y[:, wide : wide + len(ids_q)] = sin_y.T
    cos_x, sin_x = waves(ids_p, np.arange(total_x), total_x)
    table_x = np.concatenate((cos_x, sin_x), 0).astype(np.float32)
    pixels = M
    cos_u, sin_u = waves(np.arange(orders_p) - orders_p // 2, np.arange(pixels), pixels)
    strip = pixels // (tiles_x * tiles_y)
    row_table = np.zeros((2, tiles_x * tiles_y, strip, wide), np.float32)
    row_table[0, :, :, :orders_p] = (cos_u.T / math.sqrt(orders_p)).reshape(-1, strip, orders_p)
    row_table[1, :, :, :orders_p] = (sin_u.T / math.sqrt(orders_p)).reshape(-1, strip, orders_p)
    cos_v, sin_v = waves(np.arange(orders_q) - orders_q // 2, np.arange(pixels), pixels)
    g_matrix = np.zeros((2 * pixels, 2 * wide), np.float32)
    g_matrix[:pixels, :orders_q] = cos_v.T / math.sqrt(orders_q)
    g_matrix[pixels:, :orders_q] = sin_v.T / math.sqrt(orders_q)
    g_matrix[:pixels, wide : wide + orders_q] = -sin_v.T / math.sqrt(orders_q)
    g_matrix[pixels:, wide : wide + orders_q] = cos_v.T / math.sqrt(orders_q)
    g_matrix = g_matrix.astype(jnp.bfloat16)

    pieces = [phase] + [cyclic(phase, "gy", by) for by in range(1, tiles_y)]
    part, final = call(
        functools.partial(along_y_kernel, count=tiles_y),
        [(piece, "v") for piece in pieces]
        + [(jnp.asarray(table_y.reshape(tiles_y, lanes, 2 * wide)), "c"), (final, "v")],
        [shape(2 * cells_x, 2 * wide), jax.ShapeDtypeStruct(final.shape, F32)],
        [pltpu.SemaphoreType.DMA],
    )
    parts = [part] + [cyclic(part, "gx", by) for by in range(1, tiles_x)]

    facts = jnp.concatenate([pack[:, orders_q, 0:3] for pack in packs], 0)
    shifts = facts[:, 0:2].astype(jnp.int32)
    weights = facts[:, 2]
    strips = call(
        functools.partial(
            image_kernel,
            tiles_x=tiles_x,
            tiles_y=tiles_y,
            cells_x=cells_x,
            scaling=1.0 / math.sqrt(total_x * total_y * STEPS),
            sources_all=local * tiles_x * tiles_y,
        ),
        [(piece, "v") for piece in parts]
        + [(pack, "v") for pack in packs]
        + [(jnp.asarray(table_x), "c"), (jnp.asarray(g_matrix), "c"), (jnp.asarray(row_table), "c"),
           (shifts, "s"), (weights, "s")],
        [shape(strip, pixels) for _ in range(tiles_x)],
        [
            pltpu.VMEM((2, total_x, 2 * wide), F32),
            pltpu.VMEM((4, wide, wide), F32),
            pltpu.VMEM((2, wide, wide), F32),
            pltpu.VMEM((2 * wide, 2 * wide), BF16),
            pltpu.VMEM((pixels, 4 * wide), BF16),
            pltpu.VMEM((pixels, 4 * wide), BF16),
            pltpu.VMEM((pixels, wide), F32),
        ],
    )
    image = strips[0]
    for by in range(1, tiles_x):
        image = image + cyclic(strips[by], "gx", by)
    return (final.reshape(fields.shape), image)


def solution(mesh):
    placed = (
        P("clips", None, "gx", "gy"),
        P("clips", "gx", "gy"),
        P(),
        P(),
        P(("gx", "gy"), None),
        P(("gx", "gy"), None, None),
        P(("gx", "gy")),
    )

    return jax.shard_map(
        body,
        mesh=mesh,
        in_specs=placed,
        out_specs=(P("clips", None, "gx", "gy"), P(("gx", "gy"), "clips")),
        check_vma=False,
    )
```
